32 devices in a mesh: gx: 8 (over y, x, core), gy: 4 (over z).
Axes of the slice: x: 2, y: 2, z: 4, core: 2. Of those that a mesh axis runs over, the one named last changes fastest.
Arguments:
- composition: float32 [53, 262144], P(None, ('gx', 'gy')), may hold values from -6 to 6
- particle_mass: float32 [262144], P(('gx', 'gy')), may hold values from 0.3 to 3
- particle_cell: int32 [2, 262144], P(None, ('gx', 'gy')), may hold values from 0 to 511, as said below
- particle_level: int32 [262144], P(('gx', 'gy')), may hold values from 0 to 2, as said below
- les_mean: float32 [53, 32, 512], P(None, 'gx', 'gy'), may hold values from -6 to 6
- mix_rate: float32 [32, 512], P('gx', 'gy'), may hold values from 0.1 to 3
- rate_matrix: float32 [3, 53, 53], replicated, may hold values from -0.875 to 0.875
- implicit_map: float32 [3, 53, 53], replicated, may hold values from -0.875 to 0.875
Outputs:
- updated: float32 [53, 262144], P(None, ('gx', 'gy'))
- cell_means: float32 [53, 32, 512], P(None, 'gx', 'gy')
The draws below stay inside these ranges and needn't reach their ends.
Inputs may be any that keep to these rules, and one draw needn't show every extreme that they name: `particle_cell`: row 0 is below 32 and row 1 below 512. With the cells split into blocks of 4 x 128 cells in device order (streamwise block index major), every particle's cell lies within 2 cells, in each grid direction, of the block of the device that holds the particle; the distance 2 is reached on every side that has a neighbouring block. `particle_level`: the share of full-mechanism particles differs from device to device, from none to all.
All inputs are finite; a program needn't handle non-finite values.
Results may differ from the reference program's by a relative error of at most 0.0001.
Values sent between devices are 32-bit elements; how exact they have to be, the bound alone decides.
A program may use at most 64 MiB of HBM per device.

```python
import math
import jax
import jax.numpy as jnp
from jax import lax

NSP = 53
NS_LOW = 21
NS_MID = 24
CX = 4
CY = 128
R = 2
P_DEV = 8192
P_TOTAL = 262144
NX = 32
NY = 512


def draw_particle_cell(key, part):
    grid_rows = NY // CY
    device_id = jnp.arange(P_TOTAL, dtype=jnp.int32) // P_DEV
    column_index = device_id // grid_rows
    row_index = device_id % grid_rows
    key_flagx, key_flagy, key_cellx, key_celly = jax.random.split(key, 4)
    spread_x = jax.random.randint(key_flagx, (P_TOTAL,), 0, 4) == 0
    spread_y = jax.random.randint(key_flagy, (P_TOTAL,), 0, 4) == 0
    lower_x = jnp.where(spread_x, jnp.maximum(column_index * CX - R, 0), column_index * CX)
    upper_x = jnp.where(spread_x, jnp.minimum(column_index * CX + CX + R, NX), column_index * CX + CX)
    lower_y = jnp.where(spread_y, jnp.maximum(row_index * CY - R, 0), row_index * CY)
    upper_y = jnp.where(spread_y, jnp.minimum(row_index * CY + CY + R, NY), row_index * CY + CY)
    cell_x = jax.random.randint(key_cellx, (P_TOTAL,), lower_x, upper_x)
    cell_y = jax.random.randint(key_celly, (P_TOTAL,), lower_y, upper_y)
    return jnp.stack([cell_x, cell_y], 0).astype(jnp.int32)


def draw_particle_level(key, part):
    key_device, key_pick, key_lower = jax.random.split(key, 3)
    device_total = NX // CX * (NY // CY)
    flame_share = jax.random.randint(key_device, (device_total,), 0, 9)
    device_id = jnp.arange(P_TOTAL, dtype=jnp.int32) // P_DEV
    share_each = jnp.take(flame_share, device_id)
    picked = jax.random.randint(key_pick, (P_TOTAL,), 0, 8)
    lower_level = jax.random.randint(key_lower, (P_TOTAL,), 0, 2)
    return jnp.where(picked < share_each, 2, lower_level).astype(jnp.int32)


def level_of(own_key, extent, cuts, smallest, high):
    level, own = 1.0, jax.random.fold_in(own_key, 6)
    for position, shards_of in cuts:
        draws = jnp.exp(jax.random.uniform(jax.random.fold_in(own, position), (shards_of,), jnp.float32, smallest / len(cuts), high / len(cuts)))
        level = level * jnp.repeat(draws, extent[position] // shards_of).reshape([-1 if axis == position else 1 for axis in range(len(extent))])
    return level


def normal_values(rng, extent, scale, bound, cuts=(), kind=jnp.bfloat16):
    result = scale * jax.random.normal(rng, extent, jnp.float32)
    if cuts:
        result = result * level_of(rng, extent, cuts, -0.22, 0.18)
    return jnp.clip(result, -bound, bound).astype(kind)


def setup_inputs(seed: int = 0) -> dict:
    key_of = jax.random.split(jax.random.key(seed), 9)
    composition = normal_values(key_of[0], (NSP, P_TOTAL), 1.0, 6.0, ((1, 32),), jnp.float32)
    particle_mass = jnp.clip(jnp.exp(math.log(3.0) - 2.3025851 * jax.random.uniform(key_of[1], (P_TOTAL,), jnp.float32) ** level_of(key_of[1], (P_TOTAL,), ((0, 32),), -0.2, 0.2)), 0.3, 3.0)
    particle_cell = draw_particle_cell(jax.random.fold_in(key_of[8], 71), 0)
    particle_level = draw_particle_level(jax.random.fold_in(key_of[8], 71), 0)
    les_mean = normal_values(key_of[4], (NSP, NX, NY), 1.0, 6.0, ((1, 8), (2, 4)), jnp.float32)
    mix_rate = jnp.clip(jnp.exp(math.log(3.0) - 3.4011974 * jax.random.uniform(key_of[5], (NX, NY), jnp.float32) ** level_of(key_of[5], (NX, NY), ((0, 8), (1, 4)), -0.2, 0.2)), 0.1, 3.0)
    rate_matrix = normal_values(key_of[6], (3, NSP, NSP), NSP ** -0.5, 0.875, (), jnp.float32)
    implicit_map = normal_values(key_of[7], (3, NSP, NSP), NSP ** -0.5, 0.875, (), jnp.float32)
    return dict(composition=composition, particle_mass=particle_mass, particle_cell=particle_cell, particle_level=particle_level, les_mean=les_mean, mix_rate=mix_rate, rate_matrix=rate_matrix, implicit_map=implicit_map)


prior_weight = 16.0
chem_step = 0.5


def react(mixed_comp, rate_matrix, implicit_map, particle_level):
    updated = mixed_comp
    for tier_index, active in enumerate((NS_LOW, NS_MID, NSP)):
        block_comp = mixed_comp[:active]
        source = jnp.tanh(jnp.dot(rate_matrix[tier_index, :active, :active], block_comp, precision=lax.Precision.HIGHEST, preferred_element_type=jnp.float32))
        change = jnp.dot(implicit_map[tier_index, :active, :active], source, precision=lax.Precision.HIGHEST, preferred_element_type=jnp.float32)
        change = jnp.concatenate([change, jnp.zeros((NSP - active, change.shape[1]), jnp.float32)], 0)
        updated = updated + jnp.where(particle_level[None, :] == tier_index, chem_step * change, 0.0)
    return updated


def reference(composition, particle_mass, particle_cell, particle_level, les_mean, mix_rate, rate_matrix, implicit_map):
    cell_count = NX * NY
    flat_cell = (particle_cell[0] * NY + particle_cell[1]).astype(jnp.int32)
    weighted = composition * particle_mass[None, :]
    weighted_sums = jax.ops.segment_sum(weighted.T, flat_cell, num_segments=cell_count).T.reshape(NSP, NX, NY)
    mass_sums = jax.ops.segment_sum(particle_mass, flat_cell, num_segments=cell_count).reshape(1, NX, NY)
    cell_means = (weighted_sums + prior_weight * les_mean) / (mass_sums + prior_weight)
    particle_means = jnp.take(cell_means.reshape(NSP, cell_count), flat_cell, axis=1)
    particle_rate = jnp.take(mix_rate.reshape(cell_count), flat_cell, axis=0)
    factor = 1.0 - jnp.exp(-particle_rate)
    mixed_comp = composition - factor[None, :] * (composition - particle_means)
    updated = react(mixed_comp, rate_matrix, implicit_map, particle_level)
    return updated, cell_means
```

```python
import functools

import jax
import jax.numpy as jnp
from jax import lax
from jax.experimental import pallas as pl
from jax.experimental.pallas import tpu as pltpu
from jax.sharding import PartitionSpec as P

NS_LOW = 21
NS_MID = 24
R = 2
W = 2 * R
HALF = 64
ROWS = 56
LANES = 128

prior_weight = 16.0
chem_step = 0.5
BF = jnp.bfloat16
F32 = jnp.float32
MESH = pl.DeviceIdType.MESH


def halves(value):
    high = value.astype(BF)
    return high, (value - high.astype(F32)).astype(BF)


def roll(value, shift):
    return pltpu.roll(value, shift % value.shape[1], 1)


def positions(cell, block_x, block_y):
    local_x = cell[0:1] - (lax.axis_index("gx") * block_x - R)
    local_y = cell[1:2] - (lax.axis_index("gy") * block_y - R)
    low_rim = local_y < W
    on_rim = low_rim | (local_y >= block_y)
    rim = jnp.where(low_rim, local_y, local_y - block_y + (block_x + 2 * R) * W) + local_x * W
    return local_x, jnp.where(on_rim, -1, local_y - R), jnp.where(on_rim, rim, -1)


def one_hot(place, rows):
    sub = lax.broadcasted_iota(jnp.int32, (rows, place.shape[1]), 0)
    same = sub.astype(F32).astype(BF) == jnp.broadcast_to(
        place.astype(F32), (rows, place.shape[1])
    ).astype(BF)
    return jnp.where(same, jnp.ones((), BF), jnp.zeros((), BF))


def sums_kernel(
    counts, steps, chunk, block_x, block_y, comp, mass, cell, les, rate, table,
    hot, hot_rim, weighted, split, acc, acc_rim,
    send, prior, from_x, from_y, from_xy, send_main, recv_main, send_rim, recv_rim,
):
    species = comp.shape[0]
    span_x = block_x + 2 * R
    side_size = span_x * W
    gx, gy = lax.axis_index("gx"), lax.axis_index("gy")
    index = pl.program_id(0)
    has = {
        -1: (gx > 0, gy > 0),
        1: (gx < counts[0] - 1, gy < counts[1] - 1),
        0: (True, True),
    }
    others = [(dx, dy) for dx in (-1, 0, 1) for dy in (-1, 0, 1) if (dx, dy) != (0, 0)]
    lane = lax.broadcasted_iota(jnp.int32, (ROWS, LANES), 1)
    row = lax.broadcasted_iota(jnp.int32, (ROWS, LANES), 0)
    inside = (lane >= R) & (lane < block_y - R)

    def present(dx, dy):
        return jnp.logical_and(has[dx][0], has[dy][1])

    def landing(dx, dy):
        if dy == 0:
            return from_x.at[(dx + 1) // 2, W]
        if dx == 0:
            return from_y.at[(dy + 1) // 2]
        return from_xy.at[(dx + 1) // 2, (dy + 1) // 2]

    def main_copy(dx):
        first = 0 if dx < 0 else block_x
        return pltpu.make_async_remote_copy(
            src_ref=send.at[pl.ds(first, W)],
            dst_ref=from_x.at[(1 - dx) // 2, pl.ds(0, W)],
            send_sem=send_main.at[(dx + 1) // 2],
            recv_sem=recv_main.at[(1 - dx) // 2],
            device_id=(gx + dx, gy),
            device_id_type=MESH,
        )

    def rim_copy(k, dx, dy):
        return pltpu.make_async_remote_copy(
            src_ref=send.at[span_x],
            dst_ref=landing(-dx, -dy),
            send_sem=send_rim.at[k],
            recv_sem=recv_rim.at[len(others) - 1 - k],
            device_id=(gx + dx, gy + dy),
            device_id_type=MESH,
        )

    def main_arrival(dx):
        return pltpu.make_async_remote_copy(
            src_ref=send.at[pl.ds(0, W)],
            dst_ref=from_x.at[(dx + 1) // 2, pl.ds(0, W)],
            send_sem=send_main.at[(dx + 1) // 2],
            recv_sem=recv_main.at[(dx + 1) // 2],
            device_id=(gx + dx, gy),
            device_id_type=MESH,
        )

    def rim_arrival(k, dx, dy):
        return pltpu.make_async_remote_copy(
            src_ref=send.at[span_x],
            dst_ref=landing(dx, dy),
            send_sem=send_rim.at[k],
            recv_sem=recv_rim.at[k],
            device_id=(gx + dx, gy + dy),
            device_id_type=MESH,
        )

    def masked(local_x, pairs, value):
        parts = []
        for pair in pairs:
            keep = jnp.broadcast_to(local_x // 2 == pair, (16, chunk))
            keep = jnp.where(keep, 1.0, 0.0).astype(BF)
            parts.append(value * jnp.concatenate([keep] * (2 * ROWS // 16), 0))
        return jnp.concatenate(parts, 0)

    def accumulate(total, left, right):
        total[...] += lax.dot_general(
            left, right, (((1,), (1,)), ((), ())), preferred_element_type=F32
        )

    def tile(pair, parity):
        at = (pair % (span_x // 4)) * 2 * ROWS
        cols = slice(parity * block_y, (parity + 1) * block_y)
        return acc[at : at + ROWS, cols] + acc[at + ROWS : at + 2 * ROWS, cols]

    def ready(first, last):
        for t in range(first, last):
            value = tile(t // 2, t % 2)
            if R <= t < R + block_x:
                value = value + jnp.where(inside, prior[t - R], 0.0)
            send[t] = value

    half = span_x // 4
    barrier = pltpu.get_barrier_semaphore()

    @pl.when(index == 0)
    def _():
        for dx, dy in others:
            @pl.when(present(dx, dy))
            def _():
                pl.semaphore_signal(
                    barrier, inc=1, device_id=(gx + dx, gy + dy), device_id_type=MESH
                )
        acc[...] = jnp.zeros_like(acc)
        acc_rim[...] = jnp.zeros_like(acc_rim)
        weighted[...] = jnp.zeros_like(weighted)
        prior[...] = jnp.zeros_like(prior)
        for x in range(block_x):
            prior[x, 0:species, :] = prior_weight * les[:, x, :]
            prior[x, species : species + 1, :] = jnp.full((1, block_y), prior_weight, F32)
            prior[x, species + 1 : species + 2, :] = 1.0 - jnp.exp(-rate[x : x + 1, :])
        for dx in (-1, 1):
            @pl.when(jnp.logical_not(has[dx][0]))
            def _():
                from_x[(dx + 1) // 2] = jnp.zeros((W + 1, ROWS, LANES), F32)
        for dx, dy in others:
            if dy != 0:
                @pl.when(jnp.logical_not(present(dx, dy)))
                def _():
                    landing(dx, dy)[...] = jnp.zeros((ROWS, LANES), F32)

    @pl.when(index < steps)
    def _():
        weighted[0:species, :] = comp[...] * mass[...]
        weighted[species : species + 1, :] = mass[...]
        value = weighted[...]
        high = value.astype(BF).astype(F32)
        both = jnp.concatenate([high, value - high], 0).astype(BF)
        split[index] = both
        local_x, inner, rim = positions(cell[...], block_x, block_y)
        column = jnp.where(inner < 0, -1, inner + (local_x % 2) * block_y)
        hot[index] = one_hot(column, 2 * block_y)
        hot_rim[...] = one_hot(rim, HALF)
        accumulate(acc, masked(local_x, range(half), both), hot[index])
        acc_rim[:, 0:HALF] += lax.dot_general(
            both, hot_rim[...], (((1,), (1,)), ((), ())), preferred_element_type=F32
        )

    @pl.when(index == steps - 1)
    def _():
        ready(0, W)
        rim_sum = acc_rim[0:ROWS, :] + acc_rim[ROWS:, :]
        for x in range(block_x):
            t = x + R
            low_at, high_at = t * W + R, side_size + t * W
            low, high = roll(prior[x], low_at), roll(prior[x], high_at + R)
            rim_sum += jnp.where((lane >= low_at) & (lane < low_at + R), low, 0.0)
            rim_sum += jnp.where((lane >= high_at) & (lane < high_at + R), high, 0.0)
        send[span_x] = rim_sum
        acc[...] = jnp.zeros_like(acc)
        number = (1 + (gx > 0).astype(jnp.int32) + (gx < counts[0] - 1).astype(jnp.int32)) * (
            1 + (gy > 0).astype(jnp.int32) + (gy < counts[1] - 1).astype(jnp.int32)
        ) - 1
        pl.semaphore_wait(barrier, number)

        @pl.when(has[-1][0])
        def _():
            main_copy(-1).start()

        for k, (dx, dy) in enumerate(others):
            @pl.when(present(dx, dy))
            def _():
                rim_copy(k, dx, dy).start()

    @pl.when(index >= steps)
    def _():
        at = index - steps
        local_x, _, _ = positions(cell[...], block_x, block_y)
        accumulate(acc, masked(local_x, range(half, 2 * half), split[at]), hot[at])

    @pl.when(index == 2 * steps - 1)
    def _():
        ready(W, span_x)

        @pl.when(has[1][0])
        def _():
            main_copy(1).start()

        for k, (dx, dy) in enumerate(others):
            @pl.when(present(dx, dy))
            def _():
                rim_arrival(k, dx, dy).wait_recv()

        @pl.when(has[1][0])
        def _():
            main_arrival(1).wait_recv()

        def finish(total):
            total_mass = total[species : species + 1, :]
            weight = jnp.where(total_mass > 0.0, total_mass, 1.0)
            weight = jnp.broadcast_to(weight, total.shape)
            return total / jnp.where(row < species, weight, 1.0)

        low_side = lane < side_size
        place_x = jnp.where(low_side, lane, lane - side_size)
        used = lane < 2 * side_size
        behind = used & (place_x < 2 * R * W)
        ahead = used & (place_x >= block_x * W)
        total = send[span_x]
        for dx, dy in others:
            mask = used if dx == 0 else behind if dx < 0 else ahead
            if dy != 0:
                mask = mask & (low_side if dy < 0 else jnp.logical_not(low_side))
            shift = dx * block_x * W + dy * side_size
            total = total + jnp.where(mask, roll(landing(dx, dy)[...], shift), 0.0)
        rim_value = finish(total)
        table[span_x] = rim_value

        def close(t):
            total = send[t]
            if t < W:
                total = total + from_x[0, t]
            if t >= block_x:
                total = total + from_x[1, t - block_x]
            value = finish(total)
            if R <= t < R + block_x:
                low_at, high_at = t * W + R, side_size + t * W
                value = jnp.where(lane < R, roll(rim_value, -low_at), value)
                value = jnp.where(
                    lane >= block_y - R, roll(rim_value, block_y - R - high_at), value
                )
            table[t] = value

        for t in range(W, span_x):
            close(t)

        @pl.when(has[-1][0])
        def _():
            main_arrival(-1).wait_recv()

        for t in range(W):
            close(t)
        for k, (dx, dy) in enumerate(others):
            @pl.when(present(dx, dy))
            def _():
                rim_copy(k, dx, dy).wait_send()
        for dx in (-1, 1):
            @pl.when(has[dx][0])
            def _():
                main_copy(dx).wait_send()


def stack_levels(target, plain, matrices):
    species = matrices.shape[1]
    plain[...] = jnp.zeros_like(plain)
    plain[0:species, 0:species] = matrices[2]
    plain[HALF : HALF + NS_MID, 0:NS_MID] = matrices[1, 0:NS_MID, 0:NS_MID]
    base = HALF + NS_MID
    plain[base : base + NS_LOW, 0:NS_LOW] = matrices[0, 0:NS_LOW, 0:NS_LOW]
    high, low = halves(plain[...])
    target[:, 0:HALF] = high
    target[:, HALF : 2 * HALF] = high
    target[:, 2 * HALF :] = low


def react_kernel(
    block_x, block_y, comp, cell, level, table, rate, implicit, out, means,
    left, left_rim, mixed, plain, left_rate, left_implicit,
):
    species = comp.shape[0]
    span_x = block_x + 2 * R
    piece = 2048

    @pl.when(pl.program_id(0) == 0)
    def _():
        mixed[...] = jnp.zeros_like(mixed)
        stack_levels(left_rate, plain, rate)
        stack_levels(left_implicit, plain, implicit)
        high, low = halves(table[0:span_x].reshape(span_x * ROWS, block_y))
        left[:, 0:block_y] = high
        left[:, block_y:] = low
        value = table[span_x]
        high = value.astype(BF).astype(F32)
        lane = lax.broadcasted_iota(jnp.int32, value.shape, 1)
        low = roll(value - high, HALF)
        left_rim[...] = jnp.where(lane < HALF, high, low).astype(BF)
        for x in range(block_x):
            means[:, x, :] = table[x + R, 0:species, :]

    def choose(test, yes, no):
        shape = (yes.shape[0] // 8, 8, piece)
        return jnp.where(test[None], yes.reshape(shape), no.reshape(shape)).reshape(yes.shape)

    def work(at):
        span = slice(at, at + piece)
        local_x, inner, rim = positions(cell[:, span], block_x, block_y)
        hot = one_hot(inner, block_y)
        hot_rim = one_hot(rim, HALF)
        rows = jnp.dot(left[...], jnp.concatenate([hot, hot], 0), preferred_element_type=F32)
        on_rim = jnp.dot(
            left_rim[...], jnp.concatenate([hot_rim, hot_rim], 0), preferred_element_type=F32
        )
        place = jnp.broadcast_to(local_x, (8, piece))
        parts = [rows[x * ROWS : (x + 1) * ROWS] for x in range(span_x)]
        bit = 1
        while len(parts) > 1:
            test = (place & bit) != 0
            paired = [
                choose(test, parts[i + 1], parts[i]) for i in range(0, len(parts) - 1, 2)
            ]
            parts = paired + parts[2 * len(paired) :]
            bit *= 2
        taken = choose(jnp.broadcast_to(inner, (8, piece)) < 0, on_rim, parts[0])
        factor = taken[species + 1 : species + 2]
        comp_value = comp[:, span]
        mixed[0:species, span] = comp_value - factor * (comp_value - taken[0:species])
        levels = jnp.broadcast_to(level[:, span], (8, piece))
        full, middle = levels == 2, levels == 1
        base = HALF + NS_MID

        def pick(value):
            return choose(
                full, value[0:NS_MID],
                choose(middle, value[HALF:base], value[base : base + NS_MID]),
            )

        high, low = halves(mixed[:, span])
        right = jnp.concatenate([high, low, high], 0)
        drive = jnp.dot(left_rate[...], right, preferred_element_type=F32)
        source = jnp.tanh(jnp.concatenate([pick(drive), drive[NS_MID:HALF]], 0))
        high, low = halves(source)
        right = jnp.concatenate([high, low, high], 0)
        change = jnp.dot(left_implicit[...], right, preferred_element_type=F32)
        rest = change[NS_MID:ROWS]
        rest = choose(full, rest, jnp.zeros_like(rest))
        out[0:NS_MID, span] = mixed[0:NS_MID, span] + chem_step * pick(change)
        out[NS_MID:, span] = mixed[NS_MID:species, span] + chem_step * rest[0 : species - NS_MID]

    for at in range(0, comp.shape[1], piece):
        work(at)


def per_device(
    counts, composition, particle_mass, particle_cell, particle_level,
    les_mean, mix_rate, rate_matrix, implicit_map,
):
    species, particles = composition.shape
    block_x, block_y = les_mean.shape[1], les_mean.shape[2]
    span_x = block_x + 2 * R
    whole = pl.BlockSpec(memory_space=pltpu.VMEM)
    chunk = 4096
    steps = particles // chunk
    left_rows = span_x // 4 * 2 * ROWS

    def first_pass(rows):
        return pl.BlockSpec((rows, chunk), lambda i: (0, jnp.minimum(i, steps - 1)))

    dma = pltpu.SemaphoreType.DMA
    tiles = (span_x + 1, ROWS, LANES)
    table = pl.pallas_call(
        functools.partial(sums_kernel, counts, steps, chunk, block_x, block_y),
        grid=(2 * steps,),
        out_shape=pltpu.VMEM(tiles, F32),
        in_specs=[
            first_pass(species),
            first_pass(1),
            pl.BlockSpec((2, chunk), lambda i: (0, i % steps)),
            pl.BlockSpec(les_mean.shape, lambda i: (0, 0, 0)),
            pl.BlockSpec(mix_rate.shape, lambda i: (0, 0)),
        ],
        out_specs=pl.BlockSpec(memory_space=pltpu.VMEM),
        scratch_shapes=[
            pltpu.VMEM((steps, 2 * block_y, chunk), BF),
            pltpu.VMEM((HALF, chunk), BF),
            pltpu.VMEM((ROWS, chunk), F32),
            pltpu.VMEM((steps, 2 * ROWS, chunk), BF),
            pltpu.VMEM((left_rows, 2 * block_y), F32),
            pltpu.VMEM((2 * ROWS, LANES), F32),
            pltpu.VMEM(tiles, F32),
            pltpu.VMEM((block_x, ROWS, block_y), F32),
            pltpu.VMEM((2, W + 1, ROWS, LANES), F32),
            pltpu.VMEM((2, ROWS, LANES), F32),
            pltpu.VMEM((2, 2, ROWS, LANES), F32),
            dma((2,)), dma((2,)), dma((8,)), dma((8,)),
        ],
        compiler_params=pltpu.CompilerParams(
            collective_id=0, has_side_effects=True, vmem_limit_bytes=60 << 20
        ),
    )(composition, particle_mass[None], particle_cell, les_mean, mix_rate)
    stacked = HALF + 2 * NS_MID
    chunk = 2048

    def by_chunk(rows):
        return pl.BlockSpec((rows, chunk), lambda i: (0, i))

    def fixed(array):
        return pl.BlockSpec(array.shape, lambda i: (0,) * array.ndim)

    return pl.pallas_call(
        functools.partial(react_kernel, block_x, block_y),
        grid=(particles // chunk,),
        out_shape=(
            jax.ShapeDtypeStruct(composition.shape, F32),
            jax.ShapeDtypeStruct(les_mean.shape, F32),
        ),
        in_specs=[
            by_chunk(species), by_chunk(2), by_chunk(1),
            fixed(table), fixed(rate_matrix), fixed(implicit_map),
        ],
        out_specs=(by_chunk(species), fixed(les_mean)),
        scratch_shapes=[
            pltpu.VMEM((span_x * ROWS, 2 * block_y), BF),
            pltpu.VMEM((ROWS, LANES), BF),
            pltpu.VMEM((HALF, chunk), F32),
            pltpu.VMEM((stacked, HALF), F32),
            pltpu.VMEM((stacked, 3 * HALF), BF),
            pltpu.VMEM((stacked, 3 * HALF), BF),
        ],
        compiler_params=pltpu.CompilerParams(vmem_limit_bytes=40 << 20),
    )(composition, particle_cell, particle_level[None], table, rate_matrix, implicit_map)


def solution(mesh):
    placed = (
        P(None, ("gx", "gy")),
        P(("gx", "gy")),
        P(None, ("gx", "gy")),
        P(("gx", "gy")),
        P(None, "gx", "gy"),
        P("gx", "gy"),
        P(),
        P(),
    )
    return jax.shard_map(
        functools.partial(per_device, (mesh.shape["gx"], mesh.shape["gy"])),
        mesh=mesh,
        in_specs=placed,
        out_specs=(P(None, ("gx", "gy")), P(None, "gx", "gy")),
        check_vma=False,
    )
```

```python
import functools

import jax
import jax.numpy as jnp
from jax import lax
from jax.experimental import pallas as pl
from jax.experimental.pallas import tpu as pltpu
from jax.sharding import PartitionSpec as P

NS_LOW = 21
NS_MID = 24
R = 2
W = 2 * R
HALF = 64
ROWS = 56
LANES = 128

prior_weight = 16.0
chem_step = 0.5
BF = jnp.bfloat16
F32 = jnp.float32
MESH = pl.DeviceIdType.MESH


def halves(value):
    high = value.astype(BF)
    return high, (value - high.astype(F32)).astype(BF)


def roll(value, shift):
    return pltpu.roll(value, shift % value.shape[1], 1)


def positions(cell, block_x, block_y):
    local_x = cell[0:1] - (lax.axis_index("gx") * block_x - R)
    local_y = cell[1:2] - (lax.axis_index("gy") * block_y - R)
    low_rim = local_y < W
    on_rim = low_rim | (local_y >= block_y)
    rim = jnp.where(low_rim, local_y, local_y - block_y + (block_x + 2 * R) * W) + local_x * W
    return local_x, jnp.where(on_rim, -1, local_y - R), jnp.where(on_rim, rim, -1)


def one_hot(place, rows):
    sub = lax.broadcasted_iota(jnp.int32, (rows, place.shape[1]), 0)
    same = sub.astype(F32).astype(BF) == jnp.broadcast_to(
        place.astype(F32), (rows, place.shape[1])
    ).astype(BF)
    return jnp.where(same, jnp.ones((), BF), jnp.zeros((), BF))


def sums_kernel(
    counts, steps, chunk, block_x, block_y, comp, mass, cell, les, rate, table,
    hot, hot_rim, weighted, split, acc, acc_rim,
    send, prior, from_x, from_y, from_xy, send_main, recv_main, send_rim, recv_rim,
):
    species = comp.shape[0]
    span_x = block_x + 2 * R
    side_size = span_x * W
    gx, gy = lax.axis_index("gx"), lax.axis_index("gy")
    index = pl.program_id(0)
    has = {
        -1: (gx > 0, gy > 0),
        1: (gx < counts[0] - 1, gy < counts[1] - 1),
        0: (True, True),
    }
    others = [(dx, dy) for dx in (-1, 0, 1) for dy in (-1, 0, 1) if (dx, dy) != (0, 0)]
    lane = lax.broadcasted_iota(jnp.int32, (ROWS, LANES), 1)
    row = lax.broadcasted_iota(jnp.int32, (ROWS, LANES), 0)
    inside = (lane >= R) & (lane < block_y - R)

    def present(dx, dy):
        return jnp.logical_and(has[dx][0], has[dy][1])

    def landing(dx, dy):
        if dy == 0:
            return from_x.at[(dx + 1) // 2, W]
        if dx == 0:
            return from_y.at[(dy + 1) // 2]
        return from_xy.at[(dx + 1) // 2, (dy + 1) // 2]

    def main_copy(dx):
        first = 0 if dx < 0 else block_x
        return pltpu.make_async_remote_copy(
            src_ref=send.at[pl.ds(first, W)],
            dst_ref=from_x.at[(1 - dx) // 2, pl.ds(0, W)],
            send_sem=send_main.at[(dx + 1) // 2],
            recv_sem=recv_main.at[(1 - dx) // 2],
            device_id=(gx + dx, gy),
            device_id_type=MESH,
        )

    def rim_copy(k, dx, dy):
        return pltpu.make_async_remote_copy(
            src_ref=send.at[span_x],
            dst_ref=landing(-dx, -dy),
            send_sem=send_rim.at[k],
            recv_sem=recv_rim.at[len(others) - 1 - k],
            device_id=(gx + dx, gy + dy),
            device_id_type=MESH,
        )

    def main_arrival(dx):
        return pltpu.make_async_remote_copy(
            src_ref=send.at[pl.ds(0, W)],
            dst_ref=from_x.at[(dx + 1) // 2, pl.ds(0, W)],
            send_sem=send_main.at[(dx + 1) // 2],
            recv_sem=recv_main.at[(dx + 1) // 2],
            device_id=(gx + dx, gy),
            device_id_type=MESH,
        )

    def rim_arrival(k, dx, dy):
        return pltpu.make_async_remote_copy(
            src_ref=send.at[span_x],
            dst_ref=landing(dx, dy),
            send_sem=send_rim.at[k],
            recv_sem=recv_rim.at[k],
            device_id=(gx + dx, gy + dy),
            device_id_type=MESH,
        )

    def masked(local_x, pairs, value):
        parts = []
        for pair in pairs:
            keep = jnp.broadcast_to(local_x // 2 == pair, (16, chunk))
            keep = jnp.where(keep, 1.0, 0.0).astype(BF)
            parts.append(value * jnp.concatenate([keep] * (2 * ROWS // 16), 0))
        return jnp.concatenate(parts, 0)

    def accumulate(total, left, right):
        total[...] += lax.dot_general(
            left, right, (((1,), (1,)), ((), ())), preferred_element_type=F32
        )

    def tile(pair, parity):
        at = (pair % (span_x // 4)) * 2 * ROWS
        cols = slice(parity * block_y, (parity + 1) * block_y)
        return acc[at : at + ROWS, cols] + acc[at + ROWS : at + 2 * ROWS, cols]

    def ready(first, last):
        for t in range(first, last):
            value = tile(t // 2, t % 2)
            if R <= t < R + block_x:
                value = value + jnp.where(inside, prior[t - R], 0.0)
            send[t] = value

    half = span_x // 4
    barrier = pltpu.get_barrier_semaphore()

    @pl.when(index == 0)
    def _():
        for dx, dy in others:
            @pl.when(present(dx, dy))
            def _():
                pl.semaphore_signal(
                    barrier, inc=1, device_id=(gx + dx, gy + dy), device_id_type=MESH
                )
        acc[...] = jnp.zeros_like(acc)
        acc_rim[...] = jnp.zeros_like(acc_rim)
        weighted[...] = jnp.zeros_like(weighted)
        prior[...] = jnp.zeros_like(prior)
        for x in range(block_x):
            prior[x, 0:species, :] = prior_weight * les[:, x, :]
            prior[x, species : species + 1, :] = jnp.full((1, block_y), prior_weight, F32)
            prior[x, species + 1 : species + 2, :] = 1.0 - jnp.exp(-rate[x : x + 1, :])
        for dx in (-1, 1):
            @pl.when(jnp.logical_not(has[dx][0]))
            def _():
                from_x[(dx + 1) // 2] = jnp.zeros((W + 1, ROWS, LANES), F32)
        for dx, dy in others:
            if dy != 0:
                @pl.when(jnp.logical_not(present(dx, dy)))
                def _():
                    landing(dx, dy)[...] = jnp.zeros((ROWS, LANES), F32)

    @pl.when(index < steps)
    def _():
        weighted[0:species, :] = comp[...] * mass[...]
        weighted[species : species + 1, :] = mass[...]
        value = weighted[...]
        high = value.astype(BF).astype(F32)
        both = jnp.concatenate([high, value - high], 0).astype(BF)
        split[index] = both
        local_x, inner, rim = positions(cell[...], block_x, block_y)
        column = jnp.where(inner < 0, -1, inner + (local_x % 2) * block_y)
        hot[index] = one_hot(column, 2 * block_y)
        hot_rim[...] = one_hot(rim, HALF)
        accumulate(acc, masked(local_x, range(half), both), hot[index])
        acc_rim[:, 0:HALF] += lax.dot_general(
            both, hot_rim[...], (((1,), (1,)), ((), ())), preferred_element_type=F32
        )

    @pl.when(index == steps - 1)
    def _():
        ready(0, W)
        rim_sum = acc_rim[0:ROWS, :] + acc_rim[ROWS:, :]
        for x in range(block_x):
            t = x + R
            low_at, high_at = t * W + R, side_size + t * W
            low, high = roll(prior[x], low_at), roll(prior[x], high_at + R)
            rim_sum += jnp.where((lane >= low_at) & (lane < low_at + R), low, 0.0)
            rim_sum += jnp.where((lane >= high_at) & (lane < high_at + R), high, 0.0)
        send[span_x] = rim_sum
        acc[...] = jnp.zeros_like(acc)
        number = (1 + (gx > 0).astype(jnp.int32) + (gx < counts[0] - 1).astype(jnp.int32)) * (
            1 + (gy > 0).astype(jnp.int32) + (gy < counts[1] - 1).astype(jnp.int32)
        ) - 1
        pl.semaphore_wait(barrier, number)

        @pl.when(has[-1][0])
        def _():
            main_copy(-1).start()

        for k, (dx, dy) in enumerate(others):
            @pl.when(present(dx, dy))
            def _():
                rim_copy(k, dx, dy).start()

    @pl.when(index >= steps)
    def _():
        at = index - steps
        local_x, _, _ = positions(cell[...], block_x, block_y)
        accumulate(acc, masked(local_x, range(half, 2 * half), split[at]), hot[at])

    @pl.when(index == 2 * steps - 1)
    def _():
        ready(W, span_x)

        @pl.when(has[1][0])
        def _():
            main_copy(1).start()

        for k, (dx, dy) in enumerate(others):
            @pl.when(present(dx, dy))
            def _():
                rim_arrival(k, dx, dy).wait_recv()

        @pl.when(has[1][0])
        def _():
            main_arrival(1).wait_recv()

        def finish(total):
            total_mass = total[species : species + 1, :]
            weight = jnp.where(total_mass > 0.0, total_mass, 1.0)
            weight = jnp.broadcast_to(weight, total.shape)
            return total / jnp.where(row < species, weight, 1.0)

        low_side = lane < side_size
        place_x = jnp.where(low_side, lane, lane - side_size)
        used = lane < 2 * side_size
        behind = used & (place_x < 2 * R * W)
        ahead = used & (place_x >= block_x * W)
        total = send[span_x]
        for dx, dy in others:
            mask = used if dx == 0 else behind if dx < 0 else ahead
            if dy != 0:
                mask = mask & (low_side if dy < 0 else jnp.logical_not(low_side))
            shift = dx * block_x * W + dy * side_size
            total = total + jnp.where(mask, roll(landing(dx, dy)[...], shift), 0.0)
        rim_value = finish(total)
        table[span_x] = rim_value

        def close(t):
            total = send[t]
            if t < W:
                total = total + from_x[0, t]
            if t >= block_x:
                total = total + from_x[1, t - block_x]
            value = finish(total)
            if R <= t < R + block_x:
                low_at, high_at = t * W + R, side_size + t * W
                value = jnp.where(lane < R, roll(rim_value, -low_at), value)
                value = jnp.where(
                    lane >= block_y - R, roll(rim_value, block_y - R - high_at), value
                )
            table[t] = value

        for t in range(W, span_x):
            close(t)

        @pl.when(has[-1][0])
        def _():
            main_arrival(-1).wait_recv()

        for t in range(W):
            close(t)
        for k, (dx, dy) in enumerate(others):
            @pl.when(present(dx, dy))
            def _():
                rim_copy(k, dx, dy).wait_send()
        for dx in (-1, 1):
            @pl.when(has[dx][0])
            def _():
                main_copy(dx).wait_send()


def stack_levels(plain, matrices):
    species = matrices.shape[1]
    plain[...] = jnp.zeros_like(plain)
    plain[0:species, 0:species] = matrices[2]
    plain[0:NS_MID, ROWS : ROWS + NS_MID] = matrices[1, 0:NS_MID, 0:NS_MID]
    plain[ROWS : ROWS + NS_LOW, ROWS : ROWS + NS_LOW] = matrices[0, 0:NS_LOW, 0:NS_LOW]
    high, low = halves(plain[...])
    return jnp.concatenate([high, high, low], 1)


def react_kernel(
    block_x, block_y, piece, group, comp, cell, level, table, rate, implicit, out, means,
    left, left_rim, mixed, result, plain_rate, plain_implicit, done, done_means, staged,
    source, left_rate, left_implicit,
):
    species = comp.shape[0]
    particles = comp.shape[1]
    span_x = block_x + 2 * R
    pairs = span_x // 2
    for parity in range(2):
        value = jnp.concatenate([table[2 * g + parity] for g in range(pairs)], 0)
        high, low = halves(value)
        left[:, parity * block_y : (parity + 1) * block_y] = high
        left[:, (2 + parity) * block_y : (3 + parity) * block_y] = low
    value = table[span_x]
    high = value.astype(BF).astype(F32)
    lane = lax.broadcasted_iota(jnp.int32, value.shape, 1)
    low = roll(value - high, HALF)
    left_rim[...] = jnp.where(lane < HALF, high, low).astype(BF)
    mixed[species:, :] = jnp.zeros((ROWS - species, particles), F32)
    left_rate[...] = stack_levels(plain_rate, rate)
    left_implicit[...] = stack_levels(plain_implicit, implicit)

    def choose(test, yes, no):
        shape = (yes.shape[0] // 8, 8, piece)
        return jnp.where(test[None], yes.reshape(shape), no.reshape(shape)).reshape(yes.shape)

    def act(matrix, value, full, middle):
        zero = jnp.zeros_like(value)
        slots = jnp.concatenate(
            [choose(full, value, zero), choose(full, zero[0:NS_MID], value[0:NS_MID])], 0
        )
        high, low = halves(slots)
        right = jnp.concatenate([high, low, high], 0)
        got = jnp.dot(matrix, right, preferred_element_type=F32)
        first = choose(middle, got[ROWS:], got[0:NS_MID])
        return jnp.concatenate([first, got[NS_MID:ROWS]], 0)

    def copy(k):
        span = pl.ds(k * group, group)
        return pltpu.make_async_copy(result.at[:, span], out.at[:, span], done.at[k])

    def gather(span):
        local_x, inner, rim = positions(cell[:, span], block_x, block_y)
        column = jnp.where(inner < 0, -1, inner + (local_x % 2) * block_y)
        hot = one_hot(column, 2 * block_y)
        hot_rim = one_hot(rim, HALF)
        rows = jnp.dot(left[...], jnp.concatenate([hot, hot], 0), preferred_element_type=F32)
        on_rim = jnp.dot(
            left_rim[...], jnp.concatenate([hot_rim, hot_rim], 0), preferred_element_type=F32
        )
        place = jnp.broadcast_to(local_x // 2, (8, piece))
        parts = [rows[g * ROWS : (g + 1) * ROWS] for g in range(pairs)]
        bit = 1
        while len(parts) > 1:
            test = (place & bit) != 0
            paired = [
                choose(test, parts[i + 1], parts[i]) for i in range(0, len(parts) - 1, 2)
            ]
            parts = paired + parts[2 * len(paired) :]
            bit *= 2
        taken = choose(jnp.broadcast_to(inner, (8, piece)) < 0, on_rim, parts[0])
        factor = taken[species + 1 : species + 2]
        comp_value = comp[:, span]
        mixed[0:species, span] = comp_value - factor * (comp_value - taken[0:species])

    def tests(span):
        levels = jnp.broadcast_to(level[:, span], (8, piece))
        return levels == 2, levels == 0

    def drive(span):
        source[:, span] = jnp.tanh(act(left_rate[...], mixed[:, span], *tests(span)))

    def finish(span):
        change = act(left_implicit[...], source[:, span], *tests(span))
        updated = mixed[:, span] + chem_step * change
        result[:, span] = updated[0:species]

    count = particles // piece
    spans = [slice(k * piece, (k + 1) * piece) for k in range(count)]
    for k in range(count + 2):
        if k < count:
            gather(spans[k])
        if 0 <= k - 1 < count:
            drive(spans[k - 1])
        if 0 <= k - 2:
            finish(spans[k - 2])
            if (k - 1) * piece % group == 0:
                copy((k - 1) * piece // group - 1).start()
        if k == 1:
            for x in range(block_x):
                staged[:, x, :] = table[x + R, 0:species, :]
            send_means = pltpu.make_async_copy(staged, means, done_means)
            send_means.start()
    send_means.wait()
    for k in range(particles // group):
        copy(k).wait()


def per_device(
    counts, composition, particle_mass, particle_cell, particle_level,
    les_mean, mix_rate, rate_matrix, implicit_map,
):
    species, particles = composition.shape
    block_x, block_y = les_mean.shape[1], les_mean.shape[2]
    span_x = block_x + 2 * R
    whole = pl.BlockSpec(memory_space=pltpu.VMEM)
    chunk = 4096
    steps = particles // chunk
    left_rows = span_x // 4 * 2 * ROWS

    def first_pass(rows):
        return pl.BlockSpec((rows, chunk), lambda i: (0, jnp.minimum(i, steps - 1)))

    dma = pltpu.SemaphoreType.DMA
    tiles = (span_x + 1, ROWS, LANES)
    table = pl.pallas_call(
        functools.partial(sums_kernel, counts, steps, chunk, block_x, block_y),
        grid=(2 * steps,),
        out_shape=pltpu.VMEM(tiles, F32),
        in_specs=[
            first_pass(species),
            first_pass(1),
            pl.BlockSpec((2, chunk), lambda i: (0, i % steps)),
            pl.BlockSpec(les_mean.shape, lambda i: (0, 0, 0)),
            pl.BlockSpec(mix_rate.shape, lambda i: (0, 0)),
        ],
        out_specs=pl.BlockSpec(memory_space=pltpu.VMEM),
        scratch_shapes=[
            pltpu.VMEM((steps, 2 * block_y, chunk), BF),
            pltpu.VMEM((HALF, chunk), BF),
            pltpu.VMEM((ROWS, chunk), F32),
            pltpu.VMEM((steps, 2 * ROWS, chunk), BF),
            pltpu.VMEM((left_rows, 2 * block_y), F32),
            pltpu.VMEM((2 * ROWS, LANES), F32),
            pltpu.VMEM(tiles, F32),
            pltpu.VMEM((block_x, ROWS, block_y), F32),
            pltpu.VMEM((2, W + 1, ROWS, LANES), F32),
            pltpu.VMEM((2, ROWS, LANES), F32),
            pltpu.VMEM((2, 2, ROWS, LANES), F32),
            dma((2,)), dma((2,)), dma((8,)), dma((8,)),
        ],
        compiler_params=pltpu.CompilerParams(
            collective_id=0, has_side_effects=True, vmem_limit_bytes=60 << 20
        ),
    )(composition, particle_mass[None], particle_cell, les_mean, mix_rate)
    piece = 512
    group = 2048
    return pl.pallas_call(
        functools.partial(react_kernel, block_x, block_y, piece, group),
        out_shape=(
            jax.ShapeDtypeStruct(composition.shape, F32),
            jax.ShapeDtypeStruct(les_mean.shape, F32),
        ),
        in_specs=[whole] * 6,
        out_specs=[pl.BlockSpec(memory_space=pl.ANY)] * 2,
        scratch_shapes=[
            pltpu.VMEM((span_x // 2 * ROWS, 4 * block_y), BF),
            pltpu.VMEM((ROWS, LANES), BF),
            pltpu.VMEM((ROWS, particles), F32),
            pltpu.VMEM(composition.shape, F32),
            pltpu.VMEM((ROWS + NS_MID, ROWS + NS_MID), F32),
            pltpu.VMEM((ROWS + NS_MID, ROWS + NS_MID), F32),
            dma((particles // group,)),
            dma(()),
            pltpu.VMEM(les_mean.shape, F32),
            pltpu.VMEM((ROWS, particles), F32),
            pltpu.VMEM((ROWS + NS_MID, 3 * (ROWS + NS_MID)), BF),
            pltpu.VMEM((ROWS + NS_MID, 3 * (ROWS + NS_MID)), BF),
        ],
        compiler_params=pltpu.CompilerParams(vmem_limit_bytes=40 << 20),
    )(composition, particle_cell, particle_level[None], table, rate_matrix, implicit_map)


def solution(mesh):
    placed = (
        P(None, ("gx", "gy")),
        P(("gx", "gy")),
        P(None, ("gx", "gy")),
        P(("gx", "gy")),
        P(None, "gx", "gy"),
        P("gx", "gy"),
        P(),
        P(),
    )
    return jax.shard_map(
        functools.partial(per_device, (mesh.shape["gx"], mesh.shape["gy"])),
        mesh=mesh,
        in_specs=placed,
        out_specs=(P(None, ("gx", "gy")), P(None, "gx", "gy")),
        check_vma=False,
    )
```

```python
import functools

import jax
import jax.numpy as jnp
from jax import lax
from jax.experimental import pallas as pl
from jax.experimental.pallas import tpu as pltpu
from jax.sharding import PartitionSpec as P

NS_LOW = 21
NS_MID = 24
R = 2
W = 2 * R
HALF = 64
ROWS = 56
LANES = 128

prior_weight = 16.0
chem_step = 0.5
BF = jnp.bfloat16
F32 = jnp.float32
MESH = pl.DeviceIdType.MESH


def halves(value):
    high = value.astype(BF)
    return high, (value - high.astype(F32)).astype(BF)


def roll(value, shift):
    return pltpu.roll(value, shift % value.shape[1], 1)


def positions(cell, block_x, block_y):
    local_x = cell[0:1] - (lax.axis_index("gx") * block_x - R)
    local_y = cell[1:2] - (lax.axis_index("gy") * block_y - R)
    low_rim = local_y < W
    on_rim = low_rim | (local_y >= block_y)
    rim = jnp.where(low_rim, local_y, local_y - block_y + (block_x + 2 * R) * W) + local_x * W
    return local_x, on_rim, rim, local_y - R


def one_hot(place, rows):
    sub = lax.broadcasted_iota(jnp.int32, (rows, place.shape[1]), 0)
    same = sub.astype(F32).astype(BF) == jnp.broadcast_to(
        place.astype(F32), (rows, place.shape[1])
    ).astype(BF)
    return jnp.where(same, jnp.ones((), BF), jnp.zeros((), BF))


def prior_of(x, species, les, rate):
    mass = jnp.full((1, LANES), prior_weight, F32)
    fade = 1.0 - jnp.exp(-rate[x : x + 1, :])
    rest = jnp.zeros((ROWS - species - 2, LANES), F32)
    return jnp.concatenate([prior_weight * les[:, x, :], mass, fade, rest], 0)


def sums_kernel(
    counts, chunk, block_x, block_y, comp, mass, cell_in, les_in, rate_in, table,
    data, weight, weighted, cell, les, rate, hot, both, codes, acc, send, prior, plain, from_x, from_y, from_xy,
    comp_sem, small_sem, send_main, recv_main, send_rim, recv_rim,
):
    species, particles = comp.shape
    span_x = block_x + 2 * R
    pairs = span_x // 2
    side_size = span_x * W
    tall = 2 * ROWS
    chunks = particles // chunk
    gx, gy = lax.axis_index("gx"), lax.axis_index("gy")
    upper_first = gx % 2
    has = {
        -1: (gx > 0, gy > 0),
        1: (gx < counts[0] - 1, gy < counts[1] - 1),
        0: (True, True),
    }
    others = [(dx, dy) for dx in (-1, 0, 1) for dy in (-1, 0, 1) if (dx, dy) != (0, 0)]
    lane = lax.broadcasted_iota(jnp.int32, (ROWS, LANES), 1)
    row = lax.broadcasted_iota(jnp.int32, (ROWS, LANES), 0)
    inside = (lane >= R) & (lane < block_y - R)

    def chunk_copy(k):
        span = pl.ds(k * chunk, chunk)
        return pltpu.make_async_copy(
            comp.at[:, span], data.at[:, span], comp_sem.at[k]
        )

    small = [
        pltpu.make_async_copy(cell_in, cell, small_sem.at[0]),
        pltpu.make_async_copy(mass, weight, small_sem.at[1]),
        pltpu.make_async_copy(les_in, les, small_sem.at[2]),
        pltpu.make_async_copy(rate_in, rate, small_sem.at[3]),
    ]
    small[0].start()
    small[1].start()
    for k in range(chunks):
        chunk_copy(k).start()
    small[2].start()
    small[3].start()

    def present(dx, dy):
        return jnp.logical_and(has[dx][0], has[dy][1])

    def landing(dx, dy):
        if dy == 0:
            return from_x.at[(dx + 1) // 2, W]
        if dx == 0:
            return from_y.at[(dy + 1) // 2]
        return from_xy.at[(dx + 1) // 2, (dy + 1) // 2]

    def main_copy(dx):
        first = 0 if dx < 0 else block_x
        return pltpu.make_async_remote_copy(
            src_ref=send.at[pl.ds(first, W)],
            dst_ref=from_x.at[(1 - dx) // 2, pl.ds(0, W)],
            send_sem=send_main.at[(dx + 1) // 2],
            recv_sem=recv_main.at[(1 - dx) // 2],
            device_id=(gx + dx, gy),
            device_id_type=MESH,
        )

    def rim_copy(k, dx, dy):
        return pltpu.make_async_remote_copy(
            src_ref=send.at[span_x],
            dst_ref=landing(-dx, -dy),
            send_sem=send_rim.at[k],
            recv_sem=recv_rim.at[len(others) - 1 - k],
            device_id=(gx + dx, gy + dy),
            device_id_type=MESH,
        )

    def main_arrival(dx):
        return pltpu.make_async_remote_copy(
            src_ref=send.at[pl.ds(0, W)],
            dst_ref=from_x.at[(dx + 1) // 2, pl.ds(0, W)],
            send_sem=send_main.at[(dx + 1) // 2],
            recv_sem=recv_main.at[(dx + 1) // 2],
            device_id=(gx + dx, gy),
            device_id_type=MESH,
        )

    def rim_arrival(k, dx, dy):
        return pltpu.make_async_remote_copy(
            src_ref=send.at[span_x],
            dst_ref=landing(dx, dy),
            send_sem=send_rim.at[k],
            recv_sem=recv_rim.at[k],
            device_id=(gx + dx, gy + dy),
            device_id_type=MESH,
        )

    barrier = pltpu.get_barrier_semaphore()
    for dx, dy in others:
        @pl.when(present(dx, dy))
        def _():
            pl.semaphore_signal(
                barrier, inc=1, device_id=(gx + dx, gy + dy), device_id_type=MESH
            )
    weighted[species:, :] = jnp.zeros((ROWS - species, particles), F32)
    prior[...] = jnp.zeros_like(prior)
    for dx in (-1, 1):
        @pl.when(jnp.logical_not(has[dx][0]))
        def _():
            from_x[(dx + 1) // 2] = jnp.zeros((W + 1, ROWS, LANES), F32)
    for dx, dy in others:
        if dy != 0:
            @pl.when(jnp.logical_not(present(dx, dy)))
            def _():
                landing(dx, dy)[...] = jnp.zeros((ROWS, LANES), F32)

    def add_up(start, size, groups, first, fresh):
        for part in range(2):
            span = slice(start + part * (size // 2), start + (part + 1) * (size // 2))
            code = jnp.broadcast_to(codes[:, span], (16, size // 2)).astype(BF)
            value = both[:, span]
            rows = []
            for group in groups:
                keep = jnp.where(code == group, jnp.ones((), BF), jnp.zeros((), BF))
                rows.append(value * jnp.concatenate([keep] * (tall // 16), 0))
            got = lax.dot_general(
                jnp.concatenate(rows, 0), hot[:, span], (((1,), (1,)), ((), ())),
                preferred_element_type=F32,
            )
            if fresh:
                acc[part, first : first + len(groups) * tall] = got
            else:
                acc[part, first : first + len(groups) * tall] += got

    def total_of(at, cols):
        low, high = slice(at, at + ROWS), slice(at + ROWS, at + tall)
        return (acc[0, low, cols] + acc[1, low, cols]) + (acc[0, high, cols] + acc[1, high, cols])

    def half_tiles(base, first):
        for u in range(W):
            cols = slice((u % 2) * block_y, (u % 2 + 1) * block_y)
            t = first + u
            send[t] = total_of(base + (u // 2) * tall, cols) + prior[t]

    def prepare(k):
        for at in range(k * chunk, (k + 1) * chunk, 4 * LANES):
            span = slice(at, at + 4 * LANES)
            local_x, on_rim, rim, inner = positions(cell[:, span], block_x, block_y)
            hot[:, span] = one_hot(
                jnp.where(on_rim, rim, inner + (local_x % 2) * block_y), 2 * block_y
            )
            code = jnp.where(on_rim, pairs, (local_x // 2 + upper_first * (pairs // 2)) % pairs)
            codes[:, span] = code.astype(F32)
            weighted[0:species, span] = data[:, span] * weight[:, span]
            weighted[species : species + 1, span] = weight[:, span]
            value = weighted[:, span]
            high = value.astype(BF).astype(F32)
            both[:, span] = jnp.concatenate([high, value - high], 0).astype(BF)

    def set_prior():
        small[2].wait()
        small[3].wait()
        for x in range(block_x):
            own = prior_of(x, species, les, rate)
            plain[x] = own
            prior[x + R] = jnp.where(inside, own, 0.0)

    early = list(range(pairs // 2)) + [pairs]
    late = list(range(pairs // 2, pairs))
    small[0].wait()
    small[1].wait()
    late_at = len(early) * tall
    chunk_copy(0).wait()
    prepare(0)
    for k in range(chunks):
        @pl.when(gx >= 0)
        def _():
            if k + 1 < chunks:
                chunk_copy(k + 1).wait()
            add_up(k * chunk, chunk, early, 0, k == 0)
            if k + 1 < chunks:
                prepare(k + 1)
            else:
                set_prior()

    half_tiles(0, upper_first * block_x)
    rim_sum = total_of((pairs // 2) * tall, slice(0, LANES))
    for x in range(block_x):
        t = x + R
        low_at, high_at = t * W + R, side_size + t * W
        low, high = roll(plain[x], low_at), roll(plain[x], high_at + R)
        rim_sum += jnp.where((lane >= low_at) & (lane < low_at + R), low, 0.0)
        rim_sum += jnp.where((lane >= high_at) & (lane < high_at + R), high, 0.0)
    send[span_x] = rim_sum
    number = (1 + (gx > 0).astype(jnp.int32) + (gx < counts[0] - 1).astype(jnp.int32)) * (
        1 + (gy > 0).astype(jnp.int32) + (gy < counts[1] - 1).astype(jnp.int32)
    ) - 1
    pl.semaphore_wait(barrier, number)

    @pl.when(jnp.logical_and(upper_first == 0, has[-1][0]))
    def _():
        main_copy(-1).start()

    @pl.when(jnp.logical_and(upper_first == 1, has[1][0]))
    def _():
        main_copy(1).start()

    for k, (dx, dy) in enumerate(others):
        @pl.when(present(dx, dy))
        def _():
            rim_copy(k, dx, dy).start()

    @pl.when(gx >= 0)
    def _():
        add_up(0, particles, late, late_at, True)

    half_tiles(late_at, (1 - upper_first) * block_x)

    @pl.when(jnp.logical_and(upper_first == 1, has[-1][0]))
    def _():
        main_copy(-1).start()

    @pl.when(jnp.logical_and(upper_first == 0, has[1][0]))
    def _():
        main_copy(1).start()

    for k, (dx, dy) in enumerate(others):
        @pl.when(present(dx, dy))
        def _():
            rim_arrival(k, dx, dy).wait_recv()

    def finish(total):
        total_mass = total[species : species + 1, :]
        weight = jnp.where(total_mass > 0.0, total_mass, 1.0)
        weight = jnp.broadcast_to(weight, total.shape)
        return total / jnp.where(row < species, weight, 1.0)

    low_side = lane < side_size
    place_x = jnp.where(low_side, lane, lane - side_size)
    used = lane < 2 * side_size
    behind = used & (place_x < 2 * R * W)
    ahead = used & (place_x >= block_x * W)
    total = send[span_x]
    for dx, dy in others:
        mask = used if dx == 0 else behind if dx < 0 else ahead
        if dy != 0:
            mask = mask & (low_side if dy < 0 else jnp.logical_not(low_side))
        shift = dx * block_x * W + dy * side_size
        total = total + jnp.where(mask, roll(landing(dx, dy)[...], shift), 0.0)
    rim_value = finish(total)
    table[span_x] = rim_value

    def close(t):
        side, u = t // W, t % W
        value = finish(send[t] + from_x[side, u])
        if R <= t < R + block_x:
            low_at, high_at = t * W + R, side_size + t * W
            value = jnp.where(lane < R, roll(rim_value, -low_at), value)
            value = jnp.where(
                lane >= block_y - R, roll(rim_value, block_y - R - high_at), value
            )
        table[t] = value

    def close_half(dx):
        @pl.when(has[dx][0])
        def _():
            main_arrival(dx).wait_recv()

        first = 0 if dx < 0 else W
        for t in range(first, first + W):
            close(t)

    @pl.when(upper_first == 0)
    def _():
        close_half(-1)
        close_half(1)

    @pl.when(upper_first == 1)
    def _():
        close_half(1)
        close_half(-1)

    for k, (dx, dy) in enumerate(others):
        @pl.when(present(dx, dy))
        def _():
            rim_copy(k, dx, dy).wait_send()
    for dx in (-1, 1):
        @pl.when(has[dx][0])
        def _():
            main_copy(dx).wait_send()


def stack_levels(plain, matrices):
    species = matrices.shape[1]
    plain[...] = jnp.zeros_like(plain)
    plain[0:species, 0:species] = matrices[2]
    plain[0:NS_MID, ROWS : ROWS + NS_MID] = matrices[1, 0:NS_MID, 0:NS_MID]
    plain[ROWS : ROWS + NS_LOW, ROWS : ROWS + NS_LOW] = matrices[0, 0:NS_LOW, 0:NS_LOW]
    high, low = halves(plain[...])
    return jnp.concatenate([high, high, low], 1)


def react_kernel(
    block_x, block_y, piece, group, comp, cell, level, table, rate, implicit, out, means,
    left, left_rim, mixed, result, plain_rate, plain_implicit, done, done_means, staged,
    source, left_rate, left_implicit,
):
    species = comp.shape[0]
    particles = comp.shape[1]
    span_x = block_x + 2 * R
    pairs = span_x // 2
    for parity in range(2):
        value = jnp.concatenate([table[2 * g + parity] for g in range(pairs)], 0)
        high, low = halves(value)
        left[:, parity * block_y : (parity + 1) * block_y] = high
        left[:, (2 + parity) * block_y : (3 + parity) * block_y] = low
    value = table[span_x]
    high = value.astype(BF).astype(F32)
    lane = lax.broadcasted_iota(jnp.int32, value.shape, 1)
    low = roll(value - high, HALF)
    left_rim[...] = jnp.where(lane < HALF, high, low).astype(BF)
    mixed[species:, :] = jnp.zeros((ROWS - species, particles), F32)
    left_rate[...] = stack_levels(plain_rate, rate)
    left_implicit[...] = stack_levels(plain_implicit, implicit)

    def choose(test, yes, no):
        shape = (yes.shape[0] // 8, 8, piece)
        return jnp.where(test[None], yes.reshape(shape), no.reshape(shape)).reshape(yes.shape)

    def act(matrix, value, full, middle):
        zero = jnp.zeros_like(value)
        slots = jnp.concatenate(
            [choose(full, value, zero), choose(full, zero[0:NS_MID], value[0:NS_MID])], 0
        )
        high, low = halves(slots)
        right = jnp.concatenate([high, low, high], 0)
        got = jnp.dot(matrix, right, preferred_element_type=F32)
        first = choose(middle, got[ROWS:], got[0:NS_MID])
        return jnp.concatenate([first, got[NS_MID:ROWS]], 0)

    def copy(k):
        span = pl.ds(k * group, group)
        return pltpu.make_async_copy(result.at[:, span], out.at[:, span], done.at[k])

    def gather(span):
        local_x, on_rim, rim, inner = positions(cell[:, span], block_x, block_y)
        column = jnp.where(on_rim, -1, inner + (local_x % 2) * block_y)
        rim = jnp.where(on_rim, rim, -1)
        hot = one_hot(column, 2 * block_y)
        hot_rim = one_hot(rim, HALF)
        rows = jnp.dot(left[...], jnp.concatenate([hot, hot], 0), preferred_element_type=F32)
        rim_rows = jnp.dot(
            left_rim[...], jnp.concatenate([hot_rim, hot_rim], 0), preferred_element_type=F32
        )
        place = jnp.broadcast_to(local_x // 2, (8, piece))
        parts = [rows[g * ROWS : (g + 1) * ROWS] for g in range(pairs)]
        bit = 1
        while len(parts) > 1:
            test = (place & bit) != 0
            paired = [
                choose(test, parts[i + 1], parts[i]) for i in range(0, len(parts) - 1, 2)
            ]
            parts = paired + parts[2 * len(paired) :]
            bit *= 2
        taken = choose(jnp.broadcast_to(column, (8, piece)) < 0, rim_rows, parts[0])
        factor = taken[species + 1 : species + 2]
        comp_value = comp[:, span]
        mixed[0:species, span] = comp_value - factor * (comp_value - taken[0:species])

    def tests(span):
        levels = jnp.broadcast_to(level[:, span], (8, piece))
        return levels == 2, levels == 0

    def drive(span):
        source[:, span] = jnp.tanh(act(left_rate[...], mixed[:, span], *tests(span)))

    def finish(span):
        change = act(left_implicit[...], source[:, span], *tests(span))
        updated = mixed[:, span] + chem_step * change
        result[:, span] = updated[0:species]

    count = particles // piece
    spans = [slice(k * piece, (k + 1) * piece) for k in range(count)]
    for k in range(count + 2):
        if k < count:
            gather(spans[k])
        if 0 <= k - 1 < count:
            drive(spans[k - 1])
        if 0 <= k - 2:
            finish(spans[k - 2])
            if (k - 1) * piece % group == 0:
                copy((k - 1) * piece // group - 1).start()
        if k == 1:
            for x in range(block_x):
                staged[:, x, :] = table[x + R, 0:species, :]
            send_means = pltpu.make_async_copy(staged, means, done_means)
            send_means.start()
    send_means.wait()
    for k in range(particles // group):
        copy(k).wait()


def per_device(
    counts, composition, particle_mass, particle_cell, particle_level,
    les_mean, mix_rate, rate_matrix, implicit_map,
):
    species, particles = composition.shape
    block_x, block_y = les_mean.shape[1], les_mean.shape[2]
    span_x = block_x + 2 * R
    whole = pl.BlockSpec(memory_space=pltpu.VMEM)
    chunk = 2048
    hbm = pl.BlockSpec(memory_space=pltpu.HBM)
    inputs = composition, particle_mass[None], particle_cell, les_mean, mix_rate
    stay = [pltpu.with_memory_space_constraint(x, pltpu.HBM) for x in inputs]
    dma = pltpu.SemaphoreType.DMA
    tiles = (span_x + 1, ROWS, LANES)
    table = pl.pallas_call(
        functools.partial(sums_kernel, counts, chunk, block_x, block_y),
        out_shape=pltpu.VMEM(tiles, F32),
        in_specs=[hbm] * 5,
        out_specs=whole,
        scratch_shapes=[
            pltpu.VMEM(composition.shape, F32),
            pltpu.VMEM((1, particles), F32),
            pltpu.VMEM((ROWS, particles), F32),
            pltpu.VMEM(particle_cell.shape, jnp.int32),
            pltpu.VMEM(les_mean.shape, F32),
            pltpu.VMEM(mix_rate.shape, F32),
            pltpu.VMEM((2 * block_y, particles), BF),
            pltpu.VMEM((2 * ROWS, particles), BF),
            pltpu.VMEM((1, particles), F32),
            pltpu.VMEM((2, (span_x // 2 + 1) * 2 * ROWS, 2 * block_y), F32),
            pltpu.VMEM(tiles, F32),
            pltpu.VMEM((span_x, ROWS, block_y), F32),
            pltpu.VMEM((block_x, ROWS, block_y), F32),
            pltpu.VMEM((2, W + 1, ROWS, LANES), F32),
            pltpu.VMEM((2, ROWS, LANES), F32),
            pltpu.VMEM((2, 2, ROWS, LANES), F32),
            dma((particles // chunk,)), dma((4,)), dma((2,)), dma((2,)), dma((8,)), dma((8,)),
        ],
        compiler_params=pltpu.CompilerParams(
            collective_id=0, has_side_effects=True, vmem_limit_bytes=40 << 20
        ),
    )(*stay)
    piece = 512
    group = 2048
    return pl.pallas_call(
        functools.partial(react_kernel, block_x, block_y, piece, group),
        out_shape=(
            jax.ShapeDtypeStruct(composition.shape, F32),
            jax.ShapeDtypeStruct(les_mean.shape, F32),
        ),
        in_specs=[whole] * 6,
        out_specs=[pl.BlockSpec(memory_space=pl.ANY)] * 2,
        scratch_shapes=[
            pltpu.VMEM((span_x // 2 * ROWS, 4 * block_y), BF),
            pltpu.VMEM((ROWS, LANES), BF),
            pltpu.VMEM((ROWS, particles), F32),
            pltpu.VMEM(composition.shape, F32),
            pltpu.VMEM((ROWS + NS_MID, ROWS + NS_MID), F32),
            pltpu.VMEM((ROWS + NS_MID, ROWS + NS_MID), F32),
            dma((particles // group,)),
            dma(()),
            pltpu.VMEM(les_mean.shape, F32),
            pltpu.VMEM((ROWS, particles), F32),
            pltpu.VMEM((ROWS + NS_MID, 3 * (ROWS + NS_MID)), BF),
            pltpu.VMEM((ROWS + NS_MID, 3 * (ROWS + NS_MID)), BF),
        ],
        compiler_params=pltpu.CompilerParams(vmem_limit_bytes=40 << 20),
    )(composition, particle_cell, particle_level[None], table, rate_matrix, implicit_map)


def solution(mesh):
    placed = (
        P(None, ("gx", "gy")),
        P(("gx", "gy")),
        P(None, ("gx", "gy")),
        P(("gx", "gy")),
        P(None, "gx", "gy"),
        P("gx", "gy"),
        P(),
        P(),
    )
    return jax.shard_map(
        functools.partial(per_device, (mesh.shape["gx"], mesh.shape["gy"])),
        mesh=mesh,
        in_specs=placed,
        out_specs=(P(None, ("gx", "gy")), P(None, "gx", "gy")),
        check_vma=False,
    )
```

```python
import functools

import jax
import jax.numpy as jnp
from jax import lax
from jax.experimental import pallas as pl
from jax.experimental.pallas import tpu as pltpu
from jax.sharding import PartitionSpec as P

NS_LOW = 21
NS_MID = 24
R = 2
W = 2 * R
HALF = 64
ROWS = 56
LANES = 128

prior_weight = 16.0
chem_step = 0.5
BF = jnp.bfloat16
F32 = jnp.float32
MESH = pl.DeviceIdType.MESH


def halves(value):
    high = value.astype(BF)
    return high, (value - high.astype(F32)).astype(BF)


def roll(value, shift):
    return pltpu.roll(value, shift % value.shape[1], 1)


def positions(cell, block_x, block_y):
    local_x = cell[0:1] - (lax.axis_index("gx") * block_x - R)
    local_y = cell[1:2] - (lax.axis_index("gy") * block_y - R)
    low_rim = local_y < W
    on_rim = low_rim | (local_y >= block_y)
    rim = jnp.where(low_rim, local_y, local_y - block_y + (block_x + 2 * R) * W) + local_x * W
    return local_x, on_rim, rim, local_y - R


def one_hot(place, rows):
    sub = lax.broadcasted_iota(jnp.int32, (rows, place.shape[1]), 0)
    same = sub.astype(F32).astype(BF) == jnp.broadcast_to(
        place.astype(F32), (rows, place.shape[1])
    ).astype(BF)
    return jnp.where(same, jnp.ones((), BF), jnp.zeros((), BF))


def prior_of(x, species, les, rate):
    mass = jnp.full((1, LANES), prior_weight, F32)
    fade = 1.0 - jnp.exp(-rate[x : x + 1, :])
    rest = jnp.zeros((ROWS - species - 2, LANES), F32)
    return jnp.concatenate([prior_weight * les[:, x, :], mass, fade, rest], 0)


def sums_kernel(
    counts, chunk, piece, block_x, block_y, comp, mass, cell_in, les_in, rate_in, table,
    data, weight, ending, cell, les, rate, hot, codes, masked, acc, send, prior, plain, from_x, from_y, from_xy,
    comp_sem, small_sem, send_main, recv_main, send_rim, recv_rim,
):
    species, particles = comp.shape
    span_x = block_x + 2 * R
    pairs = span_x // 2
    side_size = span_x * W
    tall = 2 * ROWS
    chunks = particles // chunk
    base8 = species // 8 * 8
    gx, gy = lax.axis_index("gx"), lax.axis_index("gy")
    upper_first = gx % 2
    has = {
        -1: (gx > 0, gy > 0),
        1: (gx < counts[0] - 1, gy < counts[1] - 1),
        0: (True, True),
    }
    others = [(dx, dy) for dx in (-1, 0, 1) for dy in (-1, 0, 1) if (dx, dy) != (0, 0)]
    lane = lax.broadcasted_iota(jnp.int32, (ROWS, LANES), 1)
    row = lax.broadcasted_iota(jnp.int32, (ROWS, LANES), 0)
    inside = (lane >= R) & (lane < block_y - R)

    def chunk_copy(k):
        span = pl.ds(k * chunk, chunk)
        return pltpu.make_async_copy(
            comp.at[:, span], data.at[:, span], comp_sem.at[k]
        )

    small = [
        pltpu.make_async_copy(cell_in, cell, small_sem.at[0]),
        pltpu.make_async_copy(mass, weight, small_sem.at[1]),
        pltpu.make_async_copy(les_in, les, small_sem.at[2]),
        pltpu.make_async_copy(rate_in, rate, small_sem.at[3]),
    ]
    small[0].start()
    small[1].start()
    for k in range(chunks):
        chunk_copy(k).start()
    small[2].start()
    small[3].start()

    def present(dx, dy):
        return jnp.logical_and(has[dx][0], has[dy][1])

    def landing(dx, dy):
        if dy == 0:
            return from_x.at[(dx + 1) // 2, W]
        if dx == 0:
            return from_y.at[(dy + 1) // 2]
        return from_xy.at[(dx + 1) // 2, (dy + 1) // 2]

    def main_copy(dx):
        first = 0 if dx < 0 else block_x
        return pltpu.make_async_remote_copy(
            src_ref=send.at[pl.ds(first, W)],
            dst_ref=from_x.at[(1 - dx) // 2, pl.ds(0, W)],
            send_sem=send_main.at[(dx + 1) // 2],
            recv_sem=recv_main.at[(1 - dx) // 2],
            device_id=(gx + dx, gy),
            device_id_type=MESH,
        )

    def rim_copy(k, dx, dy):
        return pltpu.make_async_remote_copy(
            src_ref=send.at[span_x],
            dst_ref=landing(-dx, -dy),
            send_sem=send_rim.at[k],
            recv_sem=recv_rim.at[len(others) - 1 - k],
            device_id=(gx + dx, gy + dy),
            device_id_type=MESH,
        )

    def main_arrival(dx):
        return pltpu.make_async_remote_copy(
            src_ref=send.at[pl.ds(0, W)],
            dst_ref=from_x.at[(dx + 1) // 2, pl.ds(0, W)],
            send_sem=send_main.at[(dx + 1) // 2],
            recv_sem=recv_main.at[(dx + 1) // 2],
            device_id=(gx + dx, gy),
            device_id_type=MESH,
        )

    def rim_arrival(k, dx, dy):
        return pltpu.make_async_remote_copy(
            src_ref=send.at[span_x],
            dst_ref=landing(dx, dy),
            send_sem=send_rim.at[k],
            recv_sem=recv_rim.at[k],
            device_id=(gx + dx, gy + dy),
            device_id_type=MESH,
        )

    barrier = pltpu.get_barrier_semaphore()
    for dx, dy in others:
        @pl.when(present(dx, dy))
        def _():
            pl.semaphore_signal(
                barrier, inc=1, device_id=(gx + dx, gy + dy), device_id_type=MESH
            )
    ending[species - base8 :, :] = jnp.zeros((ROWS - species, particles), F32)
    prior[...] = jnp.zeros_like(prior)
    for dx in (-1, 1):
        @pl.when(jnp.logical_not(has[dx][0]))
        def _():
            from_x[(dx + 1) // 2] = jnp.zeros((W + 1, ROWS, LANES), F32)
    for dx, dy in others:
        if dy != 0:
            @pl.when(jnp.logical_not(present(dx, dy)))
            def _():
                landing(dx, dy)[...] = jnp.zeros((ROWS, LANES), F32)

    def total_of(at, cols):
        low, high = slice(at, at + ROWS), slice(at + ROWS, at + tall)
        return acc[low, cols] + acc[high, cols]

    def half_tiles(first):
        for t in range(first, first + W):
            cols = slice((t % 2) * block_y, (t % 2 + 1) * block_y)
            send[t] = total_of(t // 2 * tall, cols) + prior[t]

    def place(at):
        span = slice(at, at + piece)
        local_x, on_rim, rim, inner = positions(cell[:, span], block_x, block_y)
        hot[:, span] = one_hot(
            jnp.where(on_rim, rim, inner + (local_x % 2) * block_y), 2 * block_y
        )
        code = jnp.where(on_rim, pairs, local_x // 2)
        codes[:, span] = code.astype(F32)

    def prepare(at):
        span = slice(at, at + piece)
        mass_here = weight[:, span]
        ending[0 : species - base8, span] = data[base8:, span] * mass_here
        ending[species - base8 : species - base8 + 1, span] = mass_here
        value = jnp.concatenate([data[0:base8, span] * mass_here, ending[:, span]], 0)
        high = value.astype(BF).astype(F32)
        value = jnp.concatenate([high, value - high], 0).astype(BF)
        code = jnp.broadcast_to(codes[:, span], (16, piece)).astype(BF)
        for group in range(pairs + 1):
            keep = jnp.where(code == group, jnp.ones((), BF), jnp.zeros((), BF))
            masked[group * tall : (group + 1) * tall, span] = value * jnp.concatenate(
                [keep] * (tall // 16), 0
            )

    def set_prior():
        small[2].wait()
        small[3].wait()
        for x in range(block_x):
            own = prior_of(x, species, les, rate)
            plain[x] = own
            prior[x + R] = jnp.where(inside, own, 0.0)

    small[0].wait()
    for at in range(0, particles, piece):
        place(at)
    small[1].wait()
    for k in range(chunks):
        chunk_copy(k).wait()
        for at in range(k * chunk, (k + 1) * chunk, piece):
            prepare(at)

    set_prior()
    acc[...] = lax.dot_general(
        masked[...], hot[...], (((1,), (1,)), ((), ())), preferred_element_type=F32
    )
    number = (1 + (gx > 0).astype(jnp.int32) + (gx < counts[0] - 1).astype(jnp.int32)) * (
        1 + (gy > 0).astype(jnp.int32) + (gy < counts[1] - 1).astype(jnp.int32)
    ) - 1
    pl.semaphore_wait(barrier, number)

    def send_half(dx):
        half_tiles(0 if dx < 0 else block_x)

        @pl.when(has[dx][0])
        def _():
            main_copy(dx).start()

    @pl.when(upper_first == 0)
    def _():
        send_half(-1)

    @pl.when(upper_first == 1)
    def _():
        send_half(1)

    rim_sum = total_of(pairs * tall, slice(0, LANES))
    for x in range(block_x):
        t = x + R
        low_at, high_at = t * W + R, side_size + t * W
        low, high = roll(plain[x], low_at), roll(plain[x], high_at + R)
        rim_sum += jnp.where((lane >= low_at) & (lane < low_at + R), low, 0.0)
        rim_sum += jnp.where((lane >= high_at) & (lane < high_at + R), high, 0.0)
    send[span_x] = rim_sum
    for k, (dx, dy) in enumerate(others):
        @pl.when(present(dx, dy))
        def _():
            rim_copy(k, dx, dy).start()

    @pl.when(upper_first == 1)
    def _():
        send_half(-1)

    @pl.when(upper_first == 0)
    def _():
        send_half(1)

    for k, (dx, dy) in enumerate(others):
        @pl.when(present(dx, dy))
        def _():
            rim_arrival(k, dx, dy).wait_recv()

    def finish(total):
        total_mass = total[species : species + 1, :]
        weight = jnp.where(total_mass > 0.0, total_mass, 1.0)
        weight = jnp.broadcast_to(weight, total.shape)
        return total / jnp.where(row < species, weight, 1.0)

    low_side = lane < side_size
    place_x = jnp.where(low_side, lane, lane - side_size)
    used = lane < 2 * side_size
    behind = used & (place_x < 2 * R * W)
    ahead = used & (place_x >= block_x * W)
    total = send[span_x]
    for dx, dy in others:
        mask = used if dx == 0 else behind if dx < 0 else ahead
        if dy != 0:
            mask = mask & (low_side if dy < 0 else jnp.logical_not(low_side))
        shift = dx * block_x * W + dy * side_size
        total = total + jnp.where(mask, roll(landing(dx, dy)[...], shift), 0.0)
    rim_value = finish(total)
    table[span_x] = rim_value

    def close(t):
        side, u = t // W, t % W
        value = finish(send[t] + from_x[side, u])
        if R <= t < R + block_x:
            low_at, high_at = t * W + R, side_size + t * W
            value = jnp.where(lane < R, roll(rim_value, -low_at), value)
            value = jnp.where(
                lane >= block_y - R, roll(rim_value, block_y - R - high_at), value
            )
        table[t] = value

    def close_half(dx):
        @pl.when(has[dx][0])
        def _():
            main_arrival(dx).wait_recv()

        first = 0 if dx < 0 else W
        for t in range(first, first + W):
            close(t)

    @pl.when(upper_first == 1)
    def _():
        close_half(-1)
        close_half(1)

    @pl.when(upper_first == 0)
    def _():
        close_half(1)
        close_half(-1)

    for k, (dx, dy) in enumerate(others):
        @pl.when(present(dx, dy))
        def _():
            rim_copy(k, dx, dy).wait_send()
    for dx in (-1, 1):
        @pl.when(has[dx][0])
        def _():
            main_copy(dx).wait_send()


def stack_levels(plain, matrices):
    species = matrices.shape[1]
    plain[...] = jnp.zeros_like(plain)
    plain[0:species, 0:species] = matrices[2]
    plain[0:NS_MID, ROWS : ROWS + NS_MID] = matrices[1, 0:NS_MID, 0:NS_MID]
    plain[ROWS : ROWS + NS_LOW, ROWS : ROWS + NS_LOW] = matrices[0, 0:NS_LOW, 0:NS_LOW]
    high, low = halves(plain[...])
    return jnp.concatenate([high, high, low], 1)


def react_kernel(
    block_x, block_y, piece, group, comp, cell, level, table, rate, implicit, out, means,
    left, left_rim, mixed, result, plain_rate, plain_implicit, done, done_means, staged,
    source, left_rate, left_implicit,
):
    species = comp.shape[0]
    particles = comp.shape[1]
    span_x = block_x + 2 * R
    pairs = span_x // 2
    for parity in range(2):
        value = jnp.concatenate([table[2 * g + parity] for g in range(pairs)], 0)
        high, low = halves(value)
        left[:, parity * block_y : (parity + 1) * block_y] = high
        left[:, (2 + parity) * block_y : (3 + parity) * block_y] = low
    value = table[span_x]
    high = value.astype(BF).astype(F32)
    lane = lax.broadcasted_iota(jnp.int32, value.shape, 1)
    low = roll(value - high, HALF)
    left_rim[...] = jnp.where(lane < HALF, high, low).astype(BF)
    mixed[species:, :] = jnp.zeros((ROWS - species, particles), F32)
    left_rate[...] = stack_levels(plain_rate, rate)
    left_implicit[...] = stack_levels(plain_implicit, implicit)

    def choose(test, yes, no):
        shape = (yes.shape[0] // 8, 8, piece)
        return jnp.where(test[None], yes.reshape(shape), no.reshape(shape)).reshape(yes.shape)

    def act(matrix, value, full, middle):
        zero = jnp.zeros_like(value)
        slots = jnp.concatenate(
            [choose(full, value, zero), choose(full, zero[0:NS_MID], value[0:NS_MID])], 0
        )
        high, low = halves(slots)
        right = jnp.concatenate([high, low, high], 0)
        got = jnp.dot(matrix, right, preferred_element_type=F32)
        first = choose(middle, got[ROWS:], got[0:NS_MID])
        return jnp.concatenate([first, got[NS_MID:ROWS]], 0)

    def copy(k):
        span = pl.ds(k * group, group)
        return pltpu.make_async_copy(result.at[:, span], out.at[:, span], done.at[k])

    def gather(span):
        local_x, on_rim, rim, inner = positions(cell[:, span], block_x, block_y)
        column = jnp.where(on_rim, -1, inner + (local_x % 2) * block_y)
        rim = jnp.where(on_rim, rim, -1)
        hot = one_hot(column, 2 * block_y)
        hot_rim = one_hot(rim, HALF)
        rows = jnp.dot(left[...], jnp.concatenate([hot, hot], 0), preferred_element_type=F32)
        rim_rows = jnp.dot(
            left_rim[...], jnp.concatenate([hot_rim, hot_rim], 0), preferred_element_type=F32
        )
        place = jnp.broadcast_to(local_x // 2, (8, piece))
        parts = [rows[g * ROWS : (g + 1) * ROWS] for g in range(pairs)]
        bit = 1
        while len(parts) > 1:
            test = (place & bit) != 0
            paired = [
                choose(test, parts[i + 1], parts[i]) for i in range(0, len(parts) - 1, 2)
            ]
            parts = paired + parts[2 * len(paired) :]
            bit *= 2
        taken = choose(jnp.broadcast_to(column, (8, piece)) < 0, rim_rows, parts[0])
        factor = taken[species + 1 : species + 2]
        comp_value = comp[:, span]
        mixed[0:species, span] = comp_value - factor * (comp_value - taken[0:species])

    def tests(span):
        levels = jnp.broadcast_to(level[:, span], (8, piece))
        return levels == 2, levels == 0

    def drive(span):
        source[:, span] = jnp.tanh(act(left_rate[...], mixed[:, span], *tests(span)))

    def finish(span):
        change = act(left_implicit[...], source[:, span], *tests(span))
        updated = mixed[:, span] + chem_step * change
        result[:, span] = updated[0:species]

    count = particles // piece
    spans = [slice(k * piece, (k + 1) * piece) for k in range(count)]
    for k in range(count + 2):
        if k < count:
            gather(spans[k])
        if 0 <= k - 1 < count:
            drive(spans[k - 1])
        if 0 <= k - 2:
            finish(spans[k - 2])
            if (k - 1) * piece % group == 0:
                copy((k - 1) * piece // group - 1).start()
        if k == 1:
            for x in range(block_x):
                staged[:, x, :] = table[x + R, 0:species, :]
            send_means = pltpu.make_async_copy(staged, means, done_means)
            send_means.start()
    send_means.wait()
    for k in range(particles // group):
        copy(k).wait()


def per_device(
    counts, composition, particle_mass, particle_cell, particle_level,
    les_mean, mix_rate, rate_matrix, implicit_map,
):
    species, particles = composition.shape
    block_x, block_y = les_mean.shape[1], les_mean.shape[2]
    span_x = block_x + 2 * R
    whole = pl.BlockSpec(memory_space=pltpu.VMEM)
    chunk = 2048
    hbm = pl.BlockSpec(memory_space=pltpu.HBM)
    inputs = composition, particle_mass[None], particle_cell, les_mean, mix_rate
    stay = [pltpu.with_memory_space_constraint(x, pltpu.HBM) for x in inputs]
    dma = pltpu.SemaphoreType.DMA
    tiles = (span_x + 1, ROWS, LANES)
    table = pl.pallas_call(
        functools.partial(sums_kernel, counts, chunk, 512, block_x, block_y),
        out_shape=pltpu.VMEM(tiles, F32),
        in_specs=[hbm] * 5,
        out_specs=whole,
        scratch_shapes=[
            pltpu.VMEM(composition.shape, F32),
            pltpu.VMEM((1, particles), F32),
            pltpu.VMEM((8, particles), F32),
            pltpu.VMEM(particle_cell.shape, jnp.int32),
            pltpu.VMEM(les_mean.shape, F32),
            pltpu.VMEM(mix_rate.shape, F32),
            pltpu.VMEM((2 * block_y, particles), BF),
            pltpu.VMEM((1, particles), F32),
            pltpu.VMEM(((span_x // 2 + 1) * 2 * ROWS, particles), BF),
            pltpu.VMEM(((span_x // 2 + 1) * 2 * ROWS, 2 * block_y), F32),
            pltpu.VMEM(tiles, F32),
            pltpu.VMEM((span_x, ROWS, block_y), F32),
            pltpu.VMEM((block_x, ROWS, block_y), F32),
            pltpu.VMEM((2, W + 1, ROWS, LANES), F32),
            pltpu.VMEM((2, ROWS, LANES), F32),
            pltpu.VMEM((2, 2, ROWS, LANES), F32),
            dma((particles // chunk,)), dma((4,)), dma((2,)), dma((2,)), dma((8,)), dma((8,)),
        ],
        compiler_params=pltpu.CompilerParams(
            collective_id=0, has_side_effects=True, vmem_limit_bytes=40 << 20
        ),
    )(*stay)
    piece = 512
    group = 2048
    return pl.pallas_call(
        functools.partial(react_kernel, block_x, block_y, piece, group),
        out_shape=(
            jax.ShapeDtypeStruct(composition.shape, F32),
            jax.ShapeDtypeStruct(les_mean.shape, F32),
        ),
        in_specs=[whole] * 6,
        out_specs=[pl.BlockSpec(memory_space=pl.ANY)] * 2,
        scratch_shapes=[
            pltpu.VMEM((span_x // 2 * ROWS, 4 * block_y), BF),
            pltpu.VMEM((ROWS, LANES), BF),
            pltpu.VMEM((ROWS, particles), F32),
            pltpu.VMEM(composition.shape, F32),
            pltpu.VMEM((ROWS + NS_MID, ROWS + NS_MID), F32),
            pltpu.VMEM((ROWS + NS_MID, ROWS + NS_MID), F32),
            dma((particles // group,)),
            dma(()),
            pltpu.VMEM(les_mean.shape, F32),
            pltpu.VMEM((ROWS, particles), F32),
            pltpu.VMEM((ROWS + NS_MID, 3 * (ROWS + NS_MID)), BF),
            pltpu.VMEM((ROWS + NS_MID, 3 * (ROWS + NS_MID)), BF),
        ],
        compiler_params=pltpu.CompilerParams(vmem_limit_bytes=40 << 20),
    )(composition, particle_cell, particle_level[None], table, rate_matrix, implicit_map)


def solution(mesh):
    placed = (
        P(None, ("gx", "gy")),
        P(("gx", "gy")),
        P(None, ("gx", "gy")),
        P(("gx", "gy")),
        P(None, "gx", "gy"),
        P("gx", "gy"),
        P(),
        P(),
    )
    return jax.shard_map(
        functools.partial(per_device, (mesh.shape["gx"], mesh.shape["gy"])),
        mesh=mesh,
        in_specs=placed,
        out_specs=(P(None, ("gx", "gy")), P(None, "gx", "gy")),
        check_vma=False,
    )
```

```python
import functools

import jax
import jax.numpy as jnp
from jax import lax
from jax.experimental import pallas as pl
from jax.experimental.pallas import tpu as pltpu
from jax.sharding import PartitionSpec as P

NS_LOW = 21
NS_MID = 24
R = 2
W = 2 * R
HALF = 64
ROWS = 56
LANES = 128
FOLD = 16

prior_weight = 16.0
chem_step = 0.5
BF = jnp.bfloat16
F32 = jnp.float32
MESH = pl.DeviceIdType.MESH


def halves(value):
    high = value.astype(BF)
    return high, (value - high.astype(F32)).astype(BF)


def roll(value, shift):
    return pltpu.roll(value, shift % value.shape[1], 1)


def positions(cell, block_x, block_y):
    local_x = cell[0:1] - (lax.axis_index("gx") * block_x - R)
    local_y = cell[1:2] - (lax.axis_index("gy") * block_y - R)
    low_rim = local_y < W
    on_rim = low_rim | (local_y >= block_y)
    rim = jnp.where(low_rim, local_y, local_y - block_y + (block_x + 2 * R) * W) + local_x * W
    return local_x, on_rim, rim, local_y - R


def one_hot(place, rows):
    sub = lax.broadcasted_iota(jnp.int32, (rows, place.shape[1]), 0)
    same = sub.astype(F32).astype(BF) == jnp.broadcast_to(
        place.astype(F32), (rows, place.shape[1])
    ).astype(BF)
    return jnp.where(same, jnp.ones((), BF), jnp.zeros((), BF))


def prior_of(x, species, les, rate):
    mass = jnp.full((1, LANES), prior_weight, F32)
    fade = 1.0 - jnp.exp(-rate[x : x + 1, :])
    rest = jnp.zeros((ROWS - species - 2, LANES), F32)
    return jnp.concatenate([prior_weight * les[:, x, :], mass, fade, rest], 0)


def sums_kernel(
    counts, chunk, piece, block_x, block_y, comp, mass, cell_in, les_in, rate_in, table, data, cell,
    weight, ending, les, rate, hot, codes, masked, acc, send, edge, prior, plain, from_x, rim_x, from_y, from_xy,
    comp_sem, small_sem, send_main, recv_main, send_rim, recv_rim,
):
    species, particles = comp.shape
    span_x = block_x + 2 * R
    pairs = span_x // 2
    side_size = span_x * W
    folds = LANES // side_size
    tall = 2 * ROWS
    chunks = particles // chunk
    base8 = species // 8 * 8
    gx, gy = lax.axis_index("gx"), lax.axis_index("gy")
    upper_first = gx % 2
    has = {
        -1: (gx > 0, gy > 0),
        1: (gx < counts[0] - 1, gy < counts[1] - 1),
        0: (True, True),
    }
    others = [(dx, dy) for dx in (-1, 0, 1) for dy in (-1, 0, 1) if (dx, dy) != (0, 0)]
    lane = lax.broadcasted_iota(jnp.int32, (ROWS, LANES), 1)
    row = lax.broadcasted_iota(jnp.int32, (ROWS, LANES), 0)
    inside = (lane >= R) & (lane < block_y - R)

    def chunk_copy(k):
        span = pl.ds(k * chunk, chunk)
        return pltpu.make_async_copy(
            comp.at[:, span], data.at[:, span], comp_sem.at[k]
        )

    small = [
        pltpu.make_async_copy(cell_in, cell, small_sem.at[0]),
        pltpu.make_async_copy(mass, weight, small_sem.at[1]),
        pltpu.make_async_copy(les_in, les, small_sem.at[2]),
        pltpu.make_async_copy(rate_in, rate, small_sem.at[3]),
    ]
    small[0].start()
    small[1].start()
    for k in range(chunks):
        chunk_copy(k).start()
    small[2].start()
    small[3].start()

    def present(dx, dy):
        return jnp.logical_and(has[dx][0], has[dy][1])

    def landing(dx, dy):
        if dy == 0:
            return rim_x.at[(dx + 1) // 2]
        if dx == 0:
            return from_y.at[(dy + 1) // 2]
        return from_xy.at[(dx + 1) // 2, (dy + 1) // 2]

    def main_copy(dx):
        first = 0 if dx < 0 else block_x
        return pltpu.make_async_remote_copy(
            src_ref=send.at[pl.ds(first, W)],
            dst_ref=from_x.at[(1 - dx) // 2, pl.ds(0, W)],
            send_sem=send_main.at[(dx + 1) // 2],
            recv_sem=recv_main.at[(1 - dx) // 2],
            device_id=(gx + dx, gy),
            device_id_type=MESH,
        )

    def rim_copy(k, dx, dy):
        return pltpu.make_async_remote_copy(
            src_ref=edge if dy == 0 else edge.at[(dy + 1) // 2],
            dst_ref=landing(-dx, -dy),
            send_sem=send_rim.at[k],
            recv_sem=recv_rim.at[len(others) - 1 - k],
            device_id=(gx + dx, gy + dy),
            device_id_type=MESH,
        )

    def main_arrival(dx):
        return pltpu.make_async_remote_copy(
            src_ref=send.at[pl.ds(0, W)],
            dst_ref=from_x.at[(dx + 1) // 2, pl.ds(0, W)],
            send_sem=send_main.at[(dx + 1) // 2],
            recv_sem=recv_main.at[(dx + 1) // 2],
            device_id=(gx + dx, gy),
            device_id_type=MESH,
        )

    def rim_arrival(k, dx, dy):
        return pltpu.make_async_remote_copy(
            src_ref=edge if dy == 0 else edge.at[(dy + 1) // 2],
            dst_ref=landing(dx, dy),
            send_sem=send_rim.at[k],
            recv_sem=recv_rim.at[k],
            device_id=(gx + dx, gy + dy),
            device_id_type=MESH,
        )

    barrier = pltpu.get_barrier_semaphore()
    for dx, dy in others:
        @pl.when(present(dx, dy))
        def _():
            pl.semaphore_signal(
                barrier, inc=1, device_id=(gx + dx, gy + dy), device_id_type=MESH
            )
    ending[species - base8 :, :] = jnp.zeros((ROWS - species, particles), F32)
    prior[...] = jnp.zeros_like(prior)
    for dx in (-1, 1):
        @pl.when(jnp.logical_not(has[dx][0]))
        def _():
            from_x[(dx + 1) // 2] = jnp.zeros((W, ROWS, LANES), F32)
    for dx, dy in others:
        @pl.when(jnp.logical_not(present(dx, dy)))
        def _():
            landing(dx, dy)[...] = jnp.zeros(landing(dx, dy).shape, F32)

    def total_of(at, cols):
        low, high = slice(at, at + ROWS), slice(at + ROWS, at + tall)
        return acc[low, cols] + acc[high, cols]

    def half_tiles(first):
        for t in range(first, first + W):
            cols = slice((t % 2) * block_y, (t % 2 + 1) * block_y)
            send[t] = total_of(t // 2 * tall, cols) + prior[t]

    def place(at):
        span = slice(at, at + piece)
        local_x, on_rim, rim, inner = positions(cell[:, span], block_x, block_y)
        hot[:, span] = one_hot(
            jnp.where(on_rim, rim, inner + (local_x % 2) * block_y), 2 * block_y
        )
        code = jnp.where(on_rim, pairs, local_x // 2)
        codes[:, span] = code.astype(F32)

    def prepare(at):
        span = slice(at, at + piece)
        mass_here = weight[:, span]
        ending[0 : species - base8, span] = data[base8:, span] * mass_here
        ending[species - base8 : species - base8 + 1, span] = mass_here
        value = jnp.concatenate([data[0:base8, span] * mass_here, ending[:, span]], 0)
        high = value.astype(BF).astype(F32)
        value = jnp.concatenate([high, value - high], 0).astype(BF)
        code = jnp.broadcast_to(codes[:, span], (16, piece)).astype(BF)
        for group in range(pairs + 1):
            keep = jnp.where(code == group, jnp.ones((), BF), jnp.zeros((), BF))
            masked[group * tall : (group + 1) * tall, span] = value * jnp.concatenate(
                [keep] * (tall // 16), 0
            )

    def set_prior():
        small[2].wait()
        small[3].wait()
        for x in range(block_x):
            own = prior_of(x, species, les, rate)
            plain[x] = own
            prior[x + R] = jnp.where(inside, own, 0.0)

    small[0].wait()
    for at in range(0, particles, piece):
        place(at)
    small[1].wait()
    for k in range(chunks):
        chunk_copy(k).wait()
        for at in range(k * chunk, (k + 1) * chunk, piece):
            prepare(at)

    set_prior()
    acc[...] = lax.dot_general(
        masked[...], hot[...], (((1,), (1,)), ((), ())), preferred_element_type=F32
    )
    number = (1 + (gx > 0).astype(jnp.int32) + (gx < counts[0] - 1).astype(jnp.int32)) * (
        1 + (gy > 0).astype(jnp.int32) + (gy < counts[1] - 1).astype(jnp.int32)
    ) - 1
    pl.semaphore_wait(barrier, number)

    def send_half(dx):
        half_tiles(0 if dx < 0 else block_x)

        @pl.when(has[dx][0])
        def _():
            main_copy(dx).start()

    @pl.when(upper_first == 0)
    def _():
        send_half(-1)

    @pl.when(upper_first == 1)
    def _():
        send_half(1)

    rim_sum = total_of(pairs * tall, slice(0, LANES))
    for x in range(block_x):
        t = x + R
        low_at, high_at = t * W + R, side_size + t * W
        low, high = roll(plain[x], low_at), roll(plain[x], high_at + R)
        rim_sum += jnp.where((lane >= low_at) & (lane < low_at + R), low, 0.0)
        rim_sum += jnp.where((lane >= high_at) & (lane < high_at + R), high, 0.0)
    rim_sum = jnp.concatenate([rim_sum, jnp.zeros((folds * FOLD - ROWS, LANES), F32)], 0)
    fold_lane = lax.broadcasted_iota(jnp.int32, (FOLD, LANES), 1)
    for side in range(2):
        packed = jnp.zeros((FOLD, LANES), F32)
        for q in range(folds):
            moved = roll(rim_sum[q * FOLD : (q + 1) * FOLD], (q - side) * side_size)
            packed = jnp.where(fold_lane // side_size == q, moved, packed)
        edge[side] = packed
    for k, (dx, dy) in enumerate(others):
        @pl.when(present(dx, dy))
        def _():
            rim_copy(k, dx, dy).start()

    @pl.when(upper_first == 1)
    def _():
        send_half(-1)

    @pl.when(upper_first == 0)
    def _():
        send_half(1)

    for k, (dx, dy) in enumerate(others):
        @pl.when(present(dx, dy))
        def _():
            rim_arrival(k, dx, dy).wait_recv()

    def finish(total):
        total_mass = total[species : species + 1, :]
        weight = jnp.where(total_mass > 0.0, total_mass, 1.0)
        weight = jnp.broadcast_to(weight, total.shape)
        return total / jnp.where(row < species, weight, 1.0)

    place_x = fold_lane % side_size
    sides = []
    for side in range(2):
        total = edge[side]
        for dx, dy in others:
            if dy == 0:
                other = rim_x[(dx + 1) // 2, side]
            elif (dy + 1) // 2 == side:
                other = landing(dx, dy)[...]
            else:
                continue
            if dx < 0:
                other = jnp.where(place_x < 2 * R * W, roll(other, dx * block_x * W), 0.0)
            if dx > 0:
                other = jnp.where(place_x >= block_x * W, roll(other, dx * block_x * W), 0.0)
            total = total + other
        sides.append(total)
    parts = []
    for q in range(folds):
        low, high = roll(sides[0], -q * side_size), roll(sides[1], (1 - q) * side_size)
        parts.append(jnp.where(fold_lane < side_size, low, high))
    total = jnp.where(lane < 2 * side_size, jnp.concatenate(parts, 0)[0:ROWS], 0.0)
    rim_value = finish(total)
    table[span_x] = rim_value

    def close(t):
        side, u = t // W, t % W
        value = finish(send[t] + from_x[side, u])
        if R <= t < R + block_x:
            low_at, high_at = t * W + R, side_size + t * W
            value = jnp.where(lane < R, roll(rim_value, -low_at), value)
            value = jnp.where(
                lane >= block_y - R, roll(rim_value, block_y - R - high_at), value
            )
        table[t] = value

    def close_half(dx):
        @pl.when(has[dx][0])
        def _():
            main_arrival(dx).wait_recv()

        first = 0 if dx < 0 else W
        for t in range(first, first + W):
            close(t)

    @pl.when(upper_first == 1)
    def _():
        close_half(-1)
        close_half(1)

    @pl.when(upper_first == 0)
    def _():
        close_half(1)
        close_half(-1)

    for k, (dx, dy) in enumerate(others):
        @pl.when(present(dx, dy))
        def _():
            rim_copy(k, dx, dy).wait_send()
    for dx in (-1, 1):
        @pl.when(has[dx][0])
        def _():
            main_copy(dx).wait_send()


def stack_levels(plain, matrices):
    species = matrices.shape[1]
    plain[...] = jnp.zeros_like(plain)
    plain[0:species, 0:species] = matrices[2]
    plain[0:NS_MID, ROWS : ROWS + NS_MID] = matrices[1, 0:NS_MID, 0:NS_MID]
    plain[ROWS : ROWS + NS_LOW, ROWS : ROWS + NS_LOW] = matrices[0, 0:NS_LOW, 0:NS_LOW]
    high, low = halves(plain[...])
    return jnp.concatenate([high, high, low], 1)


def react_kernel(
    block_x, block_y, piece, group, comp, cell, level, table, rate, implicit, out, means,
    left, left_rim, mixed, result, plain_rate, plain_implicit, done, done_means, staged,
    source, left_rate, left_implicit,
):
    species = comp.shape[0]
    particles = comp.shape[1]
    span_x = block_x + 2 * R
    pairs = span_x // 2
    for parity in range(2):
        value = jnp.concatenate([table[2 * g + parity] for g in range(pairs)], 0)
        high, low = halves(value)
        left[:, parity * block_y : (parity + 1) * block_y] = high
        left[:, (2 + parity) * block_y : (3 + parity) * block_y] = low
    value = table[span_x]
    high = value.astype(BF).astype(F32)
    lane = lax.broadcasted_iota(jnp.int32, value.shape, 1)
    low = roll(value - high, HALF)
    left_rim[...] = jnp.where(lane < HALF, high, low).astype(BF)
    mixed[species:, :] = jnp.zeros((ROWS - species, particles), F32)
    left_rate[...] = stack_levels(plain_rate, rate)
    left_implicit[...] = stack_levels(plain_implicit, implicit)

    def choose(test, yes, no):
        shape = (yes.shape[0] // 8, 8, piece)
        return jnp.where(test[None], yes.reshape(shape), no.reshape(shape)).reshape(yes.shape)

    def act(matrix, value, full, middle):
        zero = jnp.zeros_like(value)
        slots = jnp.concatenate(
            [choose(full, value, zero), choose(full, zero[0:NS_MID], value[0:NS_MID])], 0
        )
        high, low = halves(slots)
        right = jnp.concatenate([high, low, high], 0)
        got = jnp.dot(matrix, right, preferred_element_type=F32)
        first = choose(middle, got[ROWS:], got[0:NS_MID])
        return jnp.concatenate([first, got[NS_MID:ROWS]], 0)

    def copy(k):
        span = pl.ds(k * group, group)
        return pltpu.make_async_copy(result.at[:, span], out.at[:, span], done.at[k])

    def gather(span):
        local_x, on_rim, rim, inner = positions(cell[:, span], block_x, block_y)
        column = jnp.where(on_rim, -1, inner + (local_x % 2) * block_y)
        rim = jnp.where(on_rim, rim, -1)
        hot = one_hot(column, 2 * block_y)
        hot_rim = one_hot(rim, HALF)
        rows = jnp.dot(left[...], jnp.concatenate([hot, hot], 0), preferred_element_type=F32)
        rim_rows = jnp.dot(
            left_rim[...], jnp.concatenate([hot_rim, hot_rim], 0), preferred_element_type=F32
        )
        place = jnp.broadcast_to(local_x // 2, (8, piece))
        parts = [rows[g * ROWS : (g + 1) * ROWS] for g in range(pairs)]
        bit = 1
        while len(parts) > 1:
            test = (place & bit) != 0
            paired = [
                choose(test, parts[i + 1], parts[i]) for i in range(0, len(parts) - 1, 2)
            ]
            parts = paired + parts[2 * len(paired) :]
            bit *= 2
        taken = choose(jnp.broadcast_to(column, (8, piece)) < 0, rim_rows, parts[0])
        factor = taken[species + 1 : species + 2]
        comp_value = comp[:, span]
        mixed[0:species, span] = comp_value - factor * (comp_value - taken[0:species])

    def tests(span):
        levels = jnp.broadcast_to(level[:, span], (8, piece))
        return levels == 2, levels == 0

    def drive(span):
        source[:, span] = jnp.tanh(act(left_rate[...], mixed[:, span], *tests(span)))

    def finish(span):
        change = act(left_implicit[...], source[:, span], *tests(span))
        updated = mixed[:, span] + chem_step * change
        result[:, span] = updated[0:species]

    count = particles // piece
    spans = [slice(k * piece, (k + 1) * piece) for k in range(count)]
    for k in range(count + 2):
        if k < count:
            gather(spans[k])
        if 0 <= k - 1 < count:
            drive(spans[k - 1])
        if 0 <= k - 2:
            finish(spans[k - 2])
            if (k - 1) * piece % group == 0:
                copy((k - 1) * piece // group - 1).start()
        if k == 1:
            for x in range(block_x):
                staged[:, x, :] = table[x + R, 0:species, :]
            send_means = pltpu.make_async_copy(staged, means, done_means)
            send_means.start()
    send_means.wait()
    for k in range(particles // group):
        copy(k).wait()


def per_device(
    counts, composition, particle_mass, particle_cell, particle_level,
    les_mean, mix_rate, rate_matrix, implicit_map,
):
    species, particles = composition.shape
    block_x, block_y = les_mean.shape[1], les_mean.shape[2]
    span_x = block_x + 2 * R
    whole = pl.BlockSpec(memory_space=pltpu.VMEM)
    chunk = 2048
    hbm = pl.BlockSpec(memory_space=pltpu.HBM)
    inputs = composition, particle_mass[None], particle_cell, les_mean, mix_rate
    stay = [pltpu.with_memory_space_constraint(x, pltpu.HBM) for x in inputs]
    dma = pltpu.SemaphoreType.DMA
    tiles = (span_x + 1, ROWS, LANES)
    table, composition, particle_cell = pl.pallas_call(
        functools.partial(sums_kernel, counts, chunk, 512, block_x, block_y),
        out_shape=(
            pltpu.VMEM(tiles, F32),
            pltpu.VMEM(composition.shape, F32),
            pltpu.VMEM(particle_cell.shape, jnp.int32),
        ),
        in_specs=[hbm] * 5,
        out_specs=[whole] * 3,
        scratch_shapes=[
            pltpu.VMEM((1, particles), F32),
            pltpu.VMEM((8, particles), F32),
            pltpu.VMEM(les_mean.shape, F32),
            pltpu.VMEM(mix_rate.shape, F32),
            pltpu.VMEM((2 * block_y, particles), BF),
            pltpu.VMEM((1, particles), F32),
            pltpu.VMEM(((span_x // 2 + 1) * 2 * ROWS, particles), BF),
            pltpu.VMEM(((span_x // 2 + 1) * 2 * ROWS, 2 * block_y), F32),
            pltpu.VMEM((span_x, ROWS, LANES), F32),
            pltpu.VMEM((2, FOLD, LANES), F32),
            pltpu.VMEM((span_x, ROWS, block_y), F32),
            pltpu.VMEM((block_x, ROWS, block_y), F32),
            pltpu.VMEM((2, W, ROWS, LANES), F32),
            pltpu.VMEM((2, 2, FOLD, LANES), F32),
            pltpu.VMEM((2, FOLD, LANES), F32),
            pltpu.VMEM((2, 2, FOLD, LANES), F32),
            dma((particles // chunk,)), dma((4,)), dma((2,)), dma((2,)), dma((8,)), dma((8,)),
        ],
        compiler_params=pltpu.CompilerParams(
            collective_id=0, has_side_effects=True, vmem_limit_bytes=40 << 20
        ),
    )(*stay)
    piece = 512
    group = 2048
    return pl.pallas_call(
        functools.partial(react_kernel, block_x, block_y, piece, group),
        out_shape=(
            jax.ShapeDtypeStruct(composition.shape, F32),
            jax.ShapeDtypeStruct(les_mean.shape, F32),
        ),
        in_specs=[whole] * 6,
        out_specs=[pl.BlockSpec(memory_space=pl.ANY)] * 2,
        scratch_shapes=[
            pltpu.VMEM((span_x // 2 * ROWS, 4 * block_y), BF),
            pltpu.VMEM((ROWS, LANES), BF),
            pltpu.VMEM((ROWS, particles), F32),
            pltpu.VMEM(composition.shape, F32),
            pltpu.VMEM((ROWS + NS_MID, ROWS + NS_MID), F32),
            pltpu.VMEM((ROWS + NS_MID, ROWS + NS_MID), F32),
            dma((particles // group,)),
            dma(()),
            pltpu.VMEM(les_mean.shape, F32),
            pltpu.VMEM((ROWS, particles), F32),
            pltpu.VMEM((ROWS + NS_MID, 3 * (ROWS + NS_MID)), BF),
            pltpu.VMEM((ROWS + NS_MID, 3 * (ROWS + NS_MID)), BF),
        ],
        compiler_params=pltpu.CompilerParams(vmem_limit_bytes=40 << 20),
    )(composition, particle_cell, particle_level[None], table, rate_matrix, implicit_map)


def solution(mesh):
    placed = (
        P(None, ("gx", "gy")),
        P(("gx", "gy")),
        P(None, ("gx", "gy")),
        P(("gx", "gy")),
        P(None, "gx", "gy"),
        P("gx", "gy"),
        P(),
        P(),
    )
    return jax.shard_map(
        functools.partial(per_device, (mesh.shape["gx"], mesh.shape["gy"])),
        mesh=mesh,
        in_specs=placed,
        out_specs=(P(None, ("gx", "gy")), P(None, "gx", "gy")),
        check_vma=False,
    )
```

```python
import functools

import jax
import jax.numpy as jnp
from jax import lax
from jax.experimental import pallas as pl
from jax.experimental.pallas import tpu as pltpu
from jax.sharding import PartitionSpec as P

NS_LOW = 21
NS_MID = 24
R = 2
W = 2 * R
HALF = 64
ROWS = 56
LANES = 128
FOLD = 16

prior_weight = 16.0
chem_step = 0.5
BF = jnp.bfloat16
F32 = jnp.float32
MESH = pl.DeviceIdType.MESH


def halves(value):
    high = value.astype(BF)
    return high, (value - high.astype(F32)).astype(BF)


def roll(value, shift):
    return pltpu.roll(value, shift % value.shape[1], 1)


def positions(cell, block_x, block_y):
    local_x = cell[0:1] - (lax.axis_index("gx") * block_x - R)
    local_y = cell[1:2] - (lax.axis_index("gy") * block_y - R)
    low_rim = local_y < W
    on_rim = low_rim | (local_y >= block_y)
    rim = jnp.where(low_rim, local_y, local_y - block_y + (block_x + 2 * R) * W) + local_x * W
    return local_x, on_rim, rim, local_y - R


def one_hot(place, rows):
    sub = lax.broadcasted_iota(jnp.int32, (rows, place.shape[1]), 0)
    same = sub.astype(F32).astype(BF) == jnp.broadcast_to(
        place.astype(F32), (rows, place.shape[1])
    ).astype(BF)
    return jnp.where(same, jnp.ones((), BF), jnp.zeros((), BF))


def prior_of(x, species, les, rate):
    mass = jnp.full((1, LANES), prior_weight, F32)
    fade = 1.0 - jnp.exp(-rate[x : x + 1, :])
    rest = jnp.zeros((ROWS - species - 2, LANES), F32)
    return jnp.concatenate([prior_weight * les[:, x, :], mass, fade, rest], 0)


def sums_kernel(
    counts, chunk, piece, block_x, block_y, comp, mass, cell_in, les_in, rate_in, table, data, cell,
    weight, ending, les, rate, hot, codes, masked, acc, send, edge, prior, plain, from_x, rim_x, from_y, from_xy,
    comp_sem, small_sem, send_main, recv_main, send_rim, recv_rim,
):
    species, particles = comp.shape
    span_x = block_x + 2 * R
    pairs = span_x // 2
    side_size = span_x * W
    folds = LANES // side_size
    tall = 2 * ROWS
    chunks = particles // chunk
    base8 = species // 8 * 8
    early = list(range(pairs // 2)) + [pairs]
    late = list(range(pairs // 2, pairs))
    rows = len(early) * tall
    gx, gy = lax.axis_index("gx"), lax.axis_index("gy")
    upper_first = gx % 2
    has = {
        -1: (gx > 0, gy > 0),
        1: (gx < counts[0] - 1, gy < counts[1] - 1),
        0: (True, True),
    }
    others = [(dx, dy) for dx in (-1, 0, 1) for dy in (-1, 0, 1) if (dx, dy) != (0, 0)]
    lane = lax.broadcasted_iota(jnp.int32, (ROWS, LANES), 1)
    row = lax.broadcasted_iota(jnp.int32, (ROWS, LANES), 0)
    inside = (lane >= R) & (lane < block_y - R)

    def chunk_copy(k):
        span = pl.ds(k * chunk, chunk)
        return pltpu.make_async_copy(
            comp.at[:, span], data.at[:, span], comp_sem.at[k]
        )

    small = [
        pltpu.make_async_copy(cell_in, cell, small_sem.at[0]),
        pltpu.make_async_copy(mass, weight, small_sem.at[1]),
        pltpu.make_async_copy(les_in, les, small_sem.at[2]),
        pltpu.make_async_copy(rate_in, rate, small_sem.at[3]),
    ]
    small[0].start()
    small[1].start()
    for k in range(chunks):
        chunk_copy(k).start()
    small[2].start()
    small[3].start()

    def present(dx, dy):
        return jnp.logical_and(has[dx][0], has[dy][1])

    def landing(dx, dy):
        if dy == 0:
            return rim_x.at[(dx + 1) // 2]
        if dx == 0:
            return from_y.at[(dy + 1) // 2]
        return from_xy.at[(dx + 1) // 2, (dy + 1) // 2]

    def main_copy(dx):
        first = 0 if dx < 0 else block_x
        return pltpu.make_async_remote_copy(
            src_ref=send.at[pl.ds(first, W)],
            dst_ref=from_x.at[(1 - dx) // 2, pl.ds(0, W)],
            send_sem=send_main.at[(dx + 1) // 2],
            recv_sem=recv_main.at[(1 - dx) // 2],
            device_id=(gx + dx, gy),
            device_id_type=MESH,
        )

    def rim_copy(k, dx, dy):
        return pltpu.make_async_remote_copy(
            src_ref=edge if dy == 0 else edge.at[(dy + 1) // 2],
            dst_ref=landing(-dx, -dy),
            send_sem=send_rim.at[k],
            recv_sem=recv_rim.at[len(others) - 1 - k],
            device_id=(gx + dx, gy + dy),
            device_id_type=MESH,
        )

    def main_arrival(dx):
        return pltpu.make_async_remote_copy(
            src_ref=send.at[pl.ds(0, W)],
            dst_ref=from_x.at[(dx + 1) // 2, pl.ds(0, W)],
            send_sem=send_main.at[(dx + 1) // 2],
            recv_sem=recv_main.at[(dx + 1) // 2],
            device_id=(gx + dx, gy),
            device_id_type=MESH,
        )

    def rim_arrival(k, dx, dy):
        return pltpu.make_async_remote_copy(
            src_ref=edge if dy == 0 else edge.at[(dy + 1) // 2],
            dst_ref=landing(dx, dy),
            send_sem=send_rim.at[k],
            recv_sem=recv_rim.at[k],
            device_id=(gx + dx, gy + dy),
            device_id_type=MESH,
        )

    barrier = pltpu.get_barrier_semaphore()
    for dx, dy in others:
        @pl.when(present(dx, dy))
        def _():
            pl.semaphore_signal(
                barrier, inc=1, device_id=(gx + dx, gy + dy), device_id_type=MESH
            )
    ending[species - base8 :, :] = jnp.zeros((ROWS - species, particles), F32)
    prior[...] = jnp.zeros_like(prior)
    masked[2 * rows - tall :, :] = jnp.zeros((tall, particles), BF)
    for dx in (-1, 1):
        @pl.when(jnp.logical_not(has[dx][0]))
        def _():
            from_x[(dx + 1) // 2] = jnp.zeros((W, ROWS, LANES), F32)
    for dx, dy in others:
        @pl.when(jnp.logical_not(present(dx, dy)))
        def _():
            landing(dx, dy)[...] = jnp.zeros(landing(dx, dy).shape, F32)

    def total_of(at, cols):
        low, high = slice(at, at + ROWS), slice(at + ROWS, at + tall)
        return acc[low, cols] + acc[high, cols]

    def half_tiles(first):
        for u in range(W):
            cols = slice((u % 2) * block_y, (u % 2 + 1) * block_y)
            send[first + u] = total_of(u // 2 * tall, cols) + prior[first + u]

    def place(at):
        span = slice(at, at + piece)
        local_x, on_rim, rim, inner = positions(cell[:, span], block_x, block_y)
        hot[:, span] = one_hot(
            jnp.where(on_rim, rim, inner + (local_x % 2) * block_y), 2 * block_y
        )
        code = jnp.where(on_rim, pairs, (local_x // 2 + upper_first * (pairs // 2)) % pairs)
        codes[:, span] = code.astype(F32)

    def prepare(at):
        span = slice(at, at + piece)
        mass_here = weight[:, span]
        ending[0 : species - base8, span] = data[base8:, span] * mass_here
        ending[species - base8 : species - base8 + 1, span] = mass_here
        value = jnp.concatenate([data[0:base8, span] * mass_here, ending[:, span]], 0)
        high = value.astype(BF).astype(F32)
        value = jnp.concatenate([high, value - high], 0).astype(BF)
        code = jnp.broadcast_to(codes[:, span], (16, piece)).astype(BF)
        for i, group in enumerate(early + late):
            keep = jnp.where(code == group, jnp.ones((), BF), jnp.zeros((), BF))
            masked[i * tall : (i + 1) * tall, span] = value * jnp.concatenate(
                [keep] * (tall // 16), 0
            )

    def set_prior():
        small[2].wait()
        small[3].wait()
        for x in range(block_x):
            own = prior_of(x, species, les, rate)
            plain[x] = own
            prior[x + R] = jnp.where(inside, own, 0.0)

    small[0].wait()
    for at in range(0, particles, piece):
        place(at)
    small[1].wait()
    for k in range(chunks):
        chunk_copy(k).wait()
        for at in range(k * chunk, (k + 1) * chunk, piece):
            prepare(at)

    set_prior()
    number = (1 + (gx > 0).astype(jnp.int32) + (gx < counts[0] - 1).astype(jnp.int32)) * (
        1 + (gy > 0).astype(jnp.int32) + (gy < counts[1] - 1).astype(jnp.int32)
    ) - 1

    @pl.loop(0, 2)
    def _(phase):
        top = pl.ds(pl.multiple_of(phase * rows, 16), rows)
        acc[...] = lax.dot_general(
            masked[top, :], hot[...], (((1,), (1,)), ((), ())), preferred_element_type=F32
        )
        half = (phase + upper_first) % 2
        half_tiles(half * block_x)

        @pl.when(phase == 0)
        def _():
            pl.semaphore_wait(barrier, number)

        for dx in (-1, 1):
            @pl.when(jnp.logical_and(half == (dx + 1) // 2, has[dx][0]))
            def _():
                main_copy(dx).start()

        @pl.when(phase == 0)
        def _():
            rim_sum = total_of(pairs // 2 * tall, slice(0, LANES))
            for x in range(block_x):
                t = x + R
                low_at, high_at = t * W + R, side_size + t * W
                low, high = roll(plain[x], low_at), roll(plain[x], high_at + R)
                rim_sum += jnp.where((lane >= low_at) & (lane < low_at + R), low, 0.0)
                rim_sum += jnp.where((lane >= high_at) & (lane < high_at + R), high, 0.0)
            rim_sum = jnp.concatenate([rim_sum, jnp.zeros((folds * FOLD - ROWS, LANES), F32)], 0)
            fold_lane = lax.broadcasted_iota(jnp.int32, (FOLD, LANES), 1)
            for side in range(2):
                packed = jnp.zeros((FOLD, LANES), F32)
                for q in range(folds):
                    moved = roll(rim_sum[q * FOLD : (q + 1) * FOLD], (q - side) * side_size)
                    packed = jnp.where(fold_lane // side_size == q, moved, packed)
                edge[side] = packed
            for k, (dx, dy) in enumerate(others):
                @pl.when(present(dx, dy))
                def _():
                    rim_copy(k, dx, dy).start()

    for k, (dx, dy) in enumerate(others):
        @pl.when(present(dx, dy))
        def _():
            rim_arrival(k, dx, dy).wait_recv()

    def finish(total):
        total_mass = total[species : species + 1, :]
        weight = jnp.where(total_mass > 0.0, total_mass, 1.0)
        weight = jnp.broadcast_to(weight, total.shape)
        return total / jnp.where(row < species, weight, 1.0)

    fold_lane = lax.broadcasted_iota(jnp.int32, (FOLD, LANES), 1)
    place_x = fold_lane % side_size
    sides = []
    for side in range(2):
        total = edge[side]
        for dx, dy in others:
            if dy == 0:
                other = rim_x[(dx + 1) // 2, side]
            elif (dy + 1) // 2 == side:
                other = landing(dx, dy)[...]
            else:
                continue
            if dx < 0:
                other = jnp.where(place_x < 2 * R * W, roll(other, dx * block_x * W), 0.0)
            if dx > 0:
                other = jnp.where(place_x >= block_x * W, roll(other, dx * block_x * W), 0.0)
            total = total + other
        sides.append(total)
    parts = []
    for q in range(folds):
        low, high = roll(sides[0], -q * side_size), roll(sides[1], (1 - q) * side_size)
        parts.append(jnp.where(fold_lane < side_size, low, high))
    total = jnp.where(lane < 2 * side_size, jnp.concatenate(parts, 0)[0:ROWS], 0.0)
    rim_value = finish(total)
    table[span_x] = rim_value

    def close(t):
        side, u = t // W, t % W
        value = finish(send[t] + from_x[side, u])
        if R <= t < R + block_x:
            low_at, high_at = t * W + R, side_size + t * W
            value = jnp.where(lane < R, roll(rim_value, -low_at), value)
            value = jnp.where(
                lane >= block_y - R, roll(rim_value, block_y - R - high_at), value
            )
        table[t] = value

    def close_half(dx):
        @pl.when(has[dx][0])
        def _():
            main_arrival(dx).wait_recv()

        first = 0 if dx < 0 else W
        for t in range(first, first + W):
            close(t)

    @pl.when(upper_first == 1)
    def _():
        close_half(-1)
        close_half(1)

    @pl.when(upper_first == 0)
    def _():
        close_half(1)
        close_half(-1)

    for k, (dx, dy) in enumerate(others):
        @pl.when(present(dx, dy))
        def _():
            rim_copy(k, dx, dy).wait_send()
    for dx in (-1, 1):
        @pl.when(has[dx][0])
        def _():
            main_copy(dx).wait_send()


def stack_levels(plain, matrices):
    species = matrices.shape[1]
    plain[...] = jnp.zeros_like(plain)
    plain[0:species, 0:species] = matrices[2]
    plain[0:NS_MID, ROWS : ROWS + NS_MID] = matrices[1, 0:NS_MID, 0:NS_MID]
    plain[ROWS : ROWS + NS_LOW, ROWS : ROWS + NS_LOW] = matrices[0, 0:NS_LOW, 0:NS_LOW]
    high, low = halves(plain[...])
    return jnp.concatenate([high, high, low], 1)


def react_kernel(
    block_x, block_y, piece, group, comp, cell, level, table, rate, implicit, out, means,
    left, left_rim, mixed, result, plain_rate, plain_implicit, done, done_means, staged,
    source, left_rate, left_implicit,
):
    species = comp.shape[0]
    particles = comp.shape[1]
    span_x = block_x + 2 * R
    pairs = span_x // 2
    for parity in range(2):
        value = jnp.concatenate([table[2 * g + parity] for g in range(pairs)], 0)
        high, low = halves(value)
        left[:, parity * block_y : (parity + 1) * block_y] = high
        left[:, (2 + parity) * block_y : (3 + parity) * block_y] = low
    value = table[span_x]
    high = value.astype(BF).astype(F32)
    lane = lax.broadcasted_iota(jnp.int32, value.shape, 1)
    low = roll(value - high, HALF)
    left_rim[...] = jnp.where(lane < HALF, high, low).astype(BF)
    mixed[species:, :] = jnp.zeros((ROWS - species, particles), F32)
    left_rate[...] = stack_levels(plain_rate, rate)
    left_implicit[...] = stack_levels(plain_implicit, implicit)

    def choose(test, yes, no):
        shape = (yes.shape[0] // 8, 8, piece)
        return jnp.where(test[None], yes.reshape(shape), no.reshape(shape)).reshape(yes.shape)

    def act(matrix, value, full, middle):
        zero = jnp.zeros_like(value)
        slots = jnp.concatenate(
            [choose(full, value, zero), choose(full, zero[0:NS_MID], value[0:NS_MID])], 0
        )
        high, low = halves(slots)
        right = jnp.concatenate([high, low, high], 0)
        got = jnp.dot(matrix, right, preferred_element_type=F32)
        first = choose(middle, got[ROWS:], got[0:NS_MID])
        return jnp.concatenate([first, got[NS_MID:ROWS]], 0)

    def copy(k):
        span = pl.ds(k * group, group)
        return pltpu.make_async_copy(result.at[:, span], out.at[:, span], done.at[k])

    def gather(span):
        local_x, on_rim, rim, inner = positions(cell[:, span], block_x, block_y)
        column = jnp.where(on_rim, -1, inner + (local_x % 2) * block_y)
        rim = jnp.where(on_rim, rim, -1)
        hot = one_hot(column, 2 * block_y)
        hot_rim = one_hot(rim, HALF)
        rows = jnp.dot(left[...], jnp.concatenate([hot, hot], 0), preferred_element_type=F32)
        rim_rows = jnp.dot(
            left_rim[...], jnp.concatenate([hot_rim, hot_rim], 0), preferred_element_type=F32
        )
        place = jnp.broadcast_to(local_x // 2, (8, piece))
        parts = [rows[g * ROWS : (g + 1) * ROWS] for g in range(pairs)]
        bit = 1
        while len(parts) > 1:
            test = (place & bit) != 0
            paired = [
                choose(test, parts[i + 1], parts[i]) for i in range(0, len(parts) - 1, 2)
            ]
            parts = paired + parts[2 * len(paired) :]
            bit *= 2
        taken = choose(jnp.broadcast_to(column, (8, piece)) < 0, rim_rows, parts[0])
        factor = taken[species + 1 : species + 2]
        comp_value = comp[:, span]
        mixed[0:species, span] = comp_value - factor * (comp_value - taken[0:species])

    def tests(span):
        levels = jnp.broadcast_to(level[:, span], (8, piece))
        return levels == 2, levels == 0

    def drive(span):
        source[:, span] = jnp.tanh(act(left_rate[...], mixed[:, span], *tests(span)))

    def finish(span):
        change = act(left_implicit[...], source[:, span], *tests(span))
        updated = mixed[:, span] + chem_step * change
        result[:, span] = updated[0:species]

    count = particles // piece
    spans = [slice(k * piece, (k + 1) * piece) for k in range(count)]
    for k in range(count + 2):
        if k < count:
            gather(spans[k])
        if 0 <= k - 1 < count:
            drive(spans[k - 1])
        if 0 <= k - 2:
            finish(spans[k - 2])
            if (k - 1) * piece % group == 0:
                copy((k - 1) * piece // group - 1).start()
        if k == 1:
            for x in range(block_x):
                staged[:, x, :] = table[x + R, 0:species, :]
            send_means = pltpu.make_async_copy(staged, means, done_means)
            send_means.start()
    send_means.wait()
    for k in range(particles // group):
        copy(k).wait()


def per_device(
    counts, composition, particle_mass, particle_cell, particle_level,
    les_mean, mix_rate, rate_matrix, implicit_map,
):
    species, particles = composition.shape
    block_x, block_y = les_mean.shape[1], les_mean.shape[2]
    span_x = block_x + 2 * R
    whole = pl.BlockSpec(memory_space=pltpu.VMEM)
    chunk = 2048
    hbm = pl.BlockSpec(memory_space=pltpu.HBM)
    inputs = composition, particle_mass[None], particle_cell, les_mean, mix_rate
    stay = [pltpu.with_memory_space_constraint(x, pltpu.HBM) for x in inputs]
    dma = pltpu.SemaphoreType.DMA
    tiles = (span_x + 1, ROWS, LANES)
    table, composition, particle_cell = pl.pallas_call(
        functools.partial(sums_kernel, counts, chunk, 512, block_x, block_y),
        out_shape=(
            pltpu.VMEM(tiles, F32),
            pltpu.VMEM(composition.shape, F32),
            pltpu.VMEM(particle_cell.shape, jnp.int32),
        ),
        in_specs=[hbm] * 5,
        out_specs=[whole] * 3,
        scratch_shapes=[
            pltpu.VMEM((1, particles), F32),
            pltpu.VMEM((8, particles), F32),
            pltpu.VMEM(les_mean.shape, F32),
            pltpu.VMEM(mix_rate.shape, F32),
            pltpu.VMEM((2 * block_y, particles), BF),
            pltpu.VMEM((1, particles), F32),
            pltpu.VMEM(((span_x // 2 + 2) * 2 * ROWS, particles), BF),
            pltpu.VMEM(((span_x // 4 + 1) * 2 * ROWS, 2 * block_y), F32),
            pltpu.VMEM((span_x, ROWS, LANES), F32),
            pltpu.VMEM((2, FOLD, LANES), F32),
            pltpu.VMEM((span_x, ROWS, block_y), F32),
            pltpu.VMEM((block_x, ROWS, block_y), F32),
            pltpu.VMEM((2, W, ROWS, LANES), F32),
            pltpu.VMEM((2, 2, FOLD, LANES), F32),
            pltpu.VMEM((2, FOLD, LANES), F32),
            pltpu.VMEM((2, 2, FOLD, LANES), F32),
            dma((particles // chunk,)), dma((4,)), dma((2,)), dma((2,)), dma((8,)), dma((8,)),
        ],
        compiler_params=pltpu.CompilerParams(
            collective_id=0, has_side_effects=True, vmem_limit_bytes=40 << 20
        ),
    )(*stay)
    piece = 512
    group = 2048
    return pl.pallas_call(
        functools.partial(react_kernel, block_x, block_y, piece, group),
        out_shape=(
            jax.ShapeDtypeStruct(composition.shape, F32),
            jax.ShapeDtypeStruct(les_mean.shape, F32),
        ),
        in_specs=[whole] * 6,
        out_specs=[pl.BlockSpec(memory_space=pl.ANY)] * 2,
        scratch_shapes=[
            pltpu.VMEM((span_x // 2 * ROWS, 4 * block_y), BF),
            pltpu.VMEM((ROWS, LANES), BF),
            pltpu.VMEM((ROWS, particles), F32),
            pltpu.VMEM(composition.shape, F32),
            pltpu.VMEM((ROWS + NS_MID, ROWS + NS_MID), F32),
            pltpu.VMEM((ROWS + NS_MID, ROWS + NS_MID), F32),
            dma((particles // group,)),
            dma(()),
            pltpu.VMEM(les_mean.shape, F32),
            pltpu.VMEM((ROWS, particles), F32),
            pltpu.VMEM((ROWS + NS_MID, 3 * (ROWS + NS_MID)), BF),
            pltpu.VMEM((ROWS + NS_MID, 3 * (ROWS + NS_MID)), BF),
        ],
        compiler_params=pltpu.CompilerParams(vmem_limit_bytes=40 << 20),
    )(composition, particle_cell, particle_level[None], table, rate_matrix, implicit_map)


def solution(mesh):
    placed = (
        P(None, ("gx", "gy")),
        P(("gx", "gy")),
        P(None, ("gx", "gy")),
        P(("gx", "gy")),
        P(None, "gx", "gy"),
        P("gx", "gy"),
        P(),
        P(),
    )
    return jax.shard_map(
        functools.partial(per_device, (mesh.shape["gx"], mesh.shape["gy"])),
        mesh=mesh,
        in_specs=placed,
        out_specs=(P(None, ("gx", "gy")), P(None, "gx", "gy")),
        check_vma=False,
    )
```

```python
import functools

import jax
import jax.numpy as jnp
from jax import lax
from jax.experimental import pallas as pl
from jax.experimental.pallas import tpu as pltpu
from jax.sharding import PartitionSpec as P

NS_LOW = 21
NS_MID = 24
R = 2
W = 2 * R
HALF = 64
ROWS = 56
LANES = 128
STACK = 112
FOLD = 16

prior_weight = 16.0
chem_step = 0.5
BF = jnp.bfloat16
F32 = jnp.float32
MESH = pl.DeviceIdType.MESH


def halves(value):
    high = value.astype(BF)
    return high, (value - high.astype(F32)).astype(BF)


def roll(value, shift):
    return pltpu.roll(value, shift % value.shape[1], 1)


def positions(cell, block_x, block_y):
    local_x = cell[0:1] - (lax.axis_index("gx") * block_x - R)
    local_y = cell[1:2] - (lax.axis_index("gy") * block_y - R)
    low_rim = local_y < W
    on_rim = low_rim | (local_y >= block_y)
    rim = jnp.where(low_rim, local_y, local_y - block_y + (block_x + 2 * R) * W) + local_x * W
    return local_x, on_rim, rim, local_y - R


def one_hot(place, rows):
    sub = lax.broadcasted_iota(jnp.int32, (rows, place.shape[1]), 0)
    same = sub.astype(F32).astype(BF) == jnp.broadcast_to(
        place.astype(F32), (rows, place.shape[1])
    ).astype(BF)
    return jnp.where(same, jnp.ones((), BF), jnp.zeros((), BF))


def prior_of(x, species, les, rate):
    mass = jnp.full((1, LANES), prior_weight, F32)
    fade = 1.0 - jnp.exp(-rate[x : x + 1, :])
    rest = jnp.zeros((ROWS - species - 2, LANES), F32)
    return jnp.concatenate([prior_weight * les[:, x, :], mass, fade, rest], 0)


def sums_kernel(
    counts, chunk, piece, block_x, block_y, comp, mass, cell_in, les_in, rate_in, table, data, cell,
    weight, ending, les, rate, hot, codes, masked, acc, send, edge, prior, plain, from_x, rim_x, from_y, from_xy,
    comp_sem, small_sem, send_main, recv_main, send_rim, recv_rim,
):
    species, particles = comp.shape
    span_x = block_x + 2 * R
    pairs = span_x // 2
    side_size = span_x * W
    folds = LANES // side_size
    tall = 2 * ROWS
    chunks = particles // chunk
    base8 = species // 8 * 8
    early = list(range(pairs // 2)) + [pairs]
    late = list(range(pairs // 2, pairs))
    rows = len(early) * tall
    gx, gy = lax.axis_index("gx"), lax.axis_index("gy")
    upper_first = gx % 2
    has = {
        -1: (gx > 0, gy > 0),
        1: (gx < counts[0] - 1, gy < counts[1] - 1),
        0: (True, True),
    }
    others = [(dx, dy) for dx in (-1, 0, 1) for dy in (-1, 0, 1) if (dx, dy) != (0, 0)]
    lane = lax.broadcasted_iota(jnp.int32, (ROWS, LANES), 1)
    row = lax.broadcasted_iota(jnp.int32, (ROWS, LANES), 0)
    inside = (lane >= R) & (lane < block_y - R)

    def chunk_copy(k):
        span = pl.ds(k * chunk, chunk)
        return pltpu.make_async_copy(
            comp.at[:, span], data.at[:, span], comp_sem.at[k]
        )

    small = [
        pltpu.make_async_copy(cell_in, cell, small_sem.at[0]),
        pltpu.make_async_copy(mass, weight, small_sem.at[1]),
        pltpu.make_async_copy(les_in, les, small_sem.at[2]),
        pltpu.make_async_copy(rate_in, rate, small_sem.at[3]),
    ]
    small[0].start()
    small[1].start()
    for k in range(chunks):
        chunk_copy(k).start()
    small[2].start()
    small[3].start()

    def present(dx, dy):
        return jnp.logical_and(has[dx][0], has[dy][1])

    def landing(dx, dy):
        if dy == 0:
            return rim_x.at[(dx + 1) // 2]
        if dx == 0:
            return from_y.at[(dy + 1) // 2]
        return from_xy.at[(dx + 1) // 2, (dy + 1) // 2]

    def main_copy(dx):
        first = 0 if dx < 0 else block_x
        return pltpu.make_async_remote_copy(
            src_ref=send.at[pl.ds(first, W)],
            dst_ref=from_x.at[(1 - dx) // 2, pl.ds(0, W)],
            send_sem=send_main.at[(dx + 1) // 2],
            recv_sem=recv_main.at[(1 - dx) // 2],
            device_id=(gx + dx, gy),
            device_id_type=MESH,
        )

    def rim_copy(k, dx, dy):
        return pltpu.make_async_remote_copy(
            src_ref=edge if dy == 0 else edge.at[(dy + 1) // 2],
            dst_ref=landing(-dx, -dy),
            send_sem=send_rim.at[k],
            recv_sem=recv_rim.at[len(others) - 1 - k],
            device_id=(gx + dx, gy + dy),
            device_id_type=MESH,
        )

    def main_arrival(dx):
        return pltpu.make_async_remote_copy(
            src_ref=send.at[pl.ds(0, W)],
            dst_ref=from_x.at[(dx + 1) // 2, pl.ds(0, W)],
            send_sem=send_main.at[(dx + 1) // 2],
            recv_sem=recv_main.at[(dx + 1) // 2],
            device_id=(gx + dx, gy),
            device_id_type=MESH,
        )

    def rim_arrival(k, dx, dy):
        return pltpu.make_async_remote_copy(
            src_ref=edge if dy == 0 else edge.at[(dy + 1) // 2],
            dst_ref=landing(dx, dy),
            send_sem=send_rim.at[k],
            recv_sem=recv_rim.at[k],
            device_id=(gx + dx, gy + dy),
            device_id_type=MESH,
        )

    barrier = pltpu.get_barrier_semaphore()
    for dx, dy in others:
        @pl.when(present(dx, dy))
        def _():
            pl.semaphore_signal(
                barrier, inc=1, device_id=(gx + dx, gy + dy), device_id_type=MESH
            )
    ending[species - base8 :, :] = jnp.zeros((ROWS - species, particles), F32)
    prior[...] = jnp.zeros_like(prior)
    masked[2 * rows - tall :, :] = jnp.zeros((tall, particles), BF)
    for dx in (-1, 1):
        @pl.when(jnp.logical_not(has[dx][0]))
        def _():
            from_x[(dx + 1) // 2] = jnp.zeros((W, ROWS, LANES), F32)
    for dx, dy in others:
        @pl.when(jnp.logical_not(present(dx, dy)))
        def _():
            landing(dx, dy)[...] = jnp.zeros(landing(dx, dy).shape, F32)

    def total_of(at, cols):
        low, high = slice(at, at + ROWS), slice(at + ROWS, at + tall)
        return acc[low, cols] + acc[high, cols]

    def half_tiles(first):
        for u in range(W):
            cols = slice((u % 2) * block_y, (u % 2 + 1) * block_y)
            send[first + u] = total_of(u // 2 * tall, cols) + prior[first + u]

    def place(at):
        span = slice(at, at + piece)
        local_x, on_rim, rim, inner = positions(cell[:, span], block_x, block_y)
        hot[:, span] = one_hot(
            jnp.where(on_rim, rim, inner + (local_x % 2) * block_y), 2 * block_y
        )
        code = jnp.where(on_rim, pairs, (local_x // 2 + upper_first * (pairs // 2)) % pairs)
        codes[:, span] = code.astype(F32)

    def prepare(at):
        span = slice(at, at + piece)
        mass_here = weight[:, span]
        ending[0 : species - base8, span] = data[base8:, span] * mass_here
        ending[species - base8 : species - base8 + 1, span] = mass_here
        value = jnp.concatenate([data[0:base8, span] * mass_here, ending[:, span]], 0)
        high = value.astype(BF).astype(F32)
        value = jnp.concatenate([high, value - high], 0).astype(BF)
        code = jnp.broadcast_to(codes[:, span], (16, piece)).astype(BF)
        for i, group in enumerate(early + late):
            keep = jnp.where(code == group, jnp.ones((), BF), jnp.zeros((), BF))
            masked[i * tall : (i + 1) * tall, span] = value * jnp.concatenate(
                [keep] * (tall // 16), 0
            )

    def set_prior():
        small[2].wait()
        small[3].wait()
        for x in range(block_x):
            own = prior_of(x, species, les, rate)
            plain[x] = own
            prior[x + R] = jnp.where(inside, own, 0.0)

    small[0].wait()
    for at in range(0, particles, piece):
        place(at)
    small[1].wait()
    for k in range(chunks):
        chunk_copy(k).wait()
        for at in range(k * chunk, (k + 1) * chunk, piece):
            prepare(at)

    set_prior()
    number = (1 + (gx > 0).astype(jnp.int32) + (gx < counts[0] - 1).astype(jnp.int32)) * (
        1 + (gy > 0).astype(jnp.int32) + (gy < counts[1] - 1).astype(jnp.int32)
    ) - 1

    @pl.loop(0, 2)
    def _(phase):
        top = pl.ds(pl.multiple_of(phase * rows, 16), rows)
        acc[...] = lax.dot_general(
            masked[top, :], hot[...], (((1,), (1,)), ((), ())), preferred_element_type=F32
        )
        half = (phase + upper_first) % 2
        half_tiles(half * block_x)

        @pl.when(phase == 0)
        def _():
            pl.semaphore_wait(barrier, number)

        for dx in (-1, 1):
            @pl.when(jnp.logical_and(half == (dx + 1) // 2, has[dx][0]))
            def _():
                main_copy(dx).start()

        @pl.when(phase == 0)
        def _():
            rim_sum = total_of(pairs // 2 * tall, slice(0, LANES))
            for x in range(block_x):
                t = x + R
                low_at, high_at = t * W + R, side_size + t * W
                low, high = roll(plain[x], low_at), roll(plain[x], high_at + R)
                rim_sum += jnp.where((lane >= low_at) & (lane < low_at + R), low, 0.0)
                rim_sum += jnp.where((lane >= high_at) & (lane < high_at + R), high, 0.0)
            rim_sum = jnp.concatenate([rim_sum, jnp.zeros((folds * FOLD - ROWS, LANES), F32)], 0)
            fold_lane = lax.broadcasted_iota(jnp.int32, (FOLD, LANES), 1)
            for side in range(2):
                packed = jnp.zeros((FOLD, LANES), F32)
                for q in range(folds):
                    moved = roll(rim_sum[q * FOLD : (q + 1) * FOLD], (q - side) * side_size)
                    packed = jnp.where(fold_lane // side_size == q, moved, packed)
                edge[side] = packed
            for k, (dx, dy) in enumerate(others):
                @pl.when(present(dx, dy))
                def _():
                    rim_copy(k, dx, dy).start()

    for k, (dx, dy) in enumerate(others):
        @pl.when(present(dx, dy))
        def _():
            rim_arrival(k, dx, dy).wait_recv()

    def finish(total):
        total_mass = total[species : species + 1, :]
        weight = jnp.where(total_mass > 0.0, total_mass, 1.0)
        weight = jnp.broadcast_to(weight, total.shape)
        return total / jnp.where(row < species, weight, 1.0)

    fold_lane = lax.broadcasted_iota(jnp.int32, (FOLD, LANES), 1)
    place_x = fold_lane % side_size
    sides = []
    for side in range(2):
        total = edge[side]
        for dx, dy in others:
            if dy == 0:
                other = rim_x[(dx + 1) // 2, side]
            elif (dy + 1) // 2 == side:
                other = landing(dx, dy)[...]
            else:
                continue
            if dx < 0:
                other = jnp.where(place_x < 2 * R * W, roll(other, dx * block_x * W), 0.0)
            if dx > 0:
                other = jnp.where(place_x >= block_x * W, roll(other, dx * block_x * W), 0.0)
            total = total + other
        sides.append(total)
    parts = []
    for q in range(folds):
        low, high = roll(sides[0], -q * side_size), roll(sides[1], (1 - q) * side_size)
        parts.append(jnp.where(fold_lane < side_size, low, high))
    total = jnp.where(lane < 2 * side_size, jnp.concatenate(parts, 0)[0:ROWS], 0.0)
    rim_value = finish(total)
    table[span_x] = rim_value

    def close(t):
        side, u = t // W, t % W
        value = finish(send[t] + from_x[side, u])
        if R <= t < R + block_x:
            low_at, high_at = t * W + R, side_size + t * W
            value = jnp.where(lane < R, roll(rim_value, -low_at), value)
            value = jnp.where(
                lane >= block_y - R, roll(rim_value, block_y - R - high_at), value
            )
        table[t] = value

    def close_half(dx):
        @pl.when(has[dx][0])
        def _():
            main_arrival(dx).wait_recv()

        first = 0 if dx < 0 else W
        for t in range(first, first + W):
            close(t)

    @pl.when(upper_first == 0)
    def _():
        close_half(-1)
        close_half(1)

    @pl.when(upper_first == 1)
    def _():
        close_half(1)
        close_half(-1)

    for k, (dx, dy) in enumerate(others):
        @pl.when(present(dx, dy))
        def _():
            rim_copy(k, dx, dy).wait_send()
    for dx in (-1, 1):
        @pl.when(has[dx][0])
        def _():
            main_copy(dx).wait_send()


def stack_levels(plain, matrices):
    species = matrices.shape[1]
    plain[...] = jnp.zeros_like(plain)
    plain[0:species, 0:species] = matrices[2]
    plain[ROWS : ROWS + NS_MID, 0:NS_MID] = matrices[1, 0:NS_MID, 0:NS_MID]
    base = ROWS + NS_MID
    plain[base : base + NS_LOW, 0:NS_LOW] = matrices[0, 0:NS_LOW, 0:NS_LOW]
    high = plain[...].astype(BF).astype(F32)
    return jnp.concatenate([high, high, plain[...] - high], 1).astype(BF)


def react_kernel(
    block_x, block_y, piece, group, comp, cell, level, table, rate, implicit, out, means,
    left, left_rim, mixed, result, plain_rate, plain_implicit, done, done_means, staged,
    source, left_rate, left_implicit,
):
    species = comp.shape[0]
    particles = comp.shape[1]
    span_x = block_x + 2 * R
    pairs = span_x // 2
    for parity in range(2):
        value = jnp.concatenate([table[2 * g + parity] for g in range(pairs)], 0)
        high, low = halves(value)
        left[:, parity * block_y : (parity + 1) * block_y] = high
        left[:, (2 + parity) * block_y : (3 + parity) * block_y] = low
    value = table[span_x]
    high = value.astype(BF).astype(F32)
    lane = lax.broadcasted_iota(jnp.int32, value.shape, 1)
    low = roll(value - high, HALF)
    left_rim[...] = jnp.where(lane < HALF, high, low).astype(BF)
    mixed[species:, :] = jnp.zeros((ROWS - species, particles), F32)
    left_rate[...] = stack_levels(plain_rate, rate)
    left_implicit[...] = stack_levels(plain_implicit, implicit)

    def choose(test, yes, no):
        shape = (yes.shape[0] // 8, 8, piece)
        return jnp.where(test[None], yes.reshape(shape), no.reshape(shape)).reshape(yes.shape)

    def act(matrix, value, full, lowest):
        high = value.astype(BF).astype(F32)
        right = jnp.concatenate([high, value - high, high], 0).astype(BF)
        got = jnp.dot(matrix, right, preferred_element_type=F32)
        base = ROWS + NS_MID
        first = choose(lowest, got[base : base + NS_MID], got[ROWS:base])
        return choose(full, got[0:NS_MID], first), got[NS_MID:ROWS]

    def copy(k):
        span = pl.ds(k * group, group)
        return pltpu.make_async_copy(result.at[:, span], out.at[:, span], done.at[k])

    def gather(span):
        local_x, on_rim, rim, inner = positions(cell[:, span], block_x, block_y)
        column = jnp.where(on_rim, -1, inner + (local_x % 2) * block_y)
        rim = jnp.where(on_rim, rim, -1)
        hot = one_hot(column, 2 * block_y)
        hot_rim = one_hot(rim, HALF)
        rows = jnp.dot(left[...], jnp.concatenate([hot, hot], 0), preferred_element_type=F32)
        rim_rows = jnp.dot(
            left_rim[...], jnp.concatenate([hot_rim, hot_rim], 0), preferred_element_type=F32
        )
        place = jnp.broadcast_to(local_x // 2, (8, piece))
        parts = [rows[g * ROWS : (g + 1) * ROWS] for g in range(pairs)]
        bit = 1
        while len(parts) > 1:
            test = (place & bit) != 0
            paired = [
                choose(test, parts[i + 1], parts[i]) for i in range(0, len(parts) - 1, 2)
            ]
            parts = paired + parts[2 * len(paired) :]
            bit *= 2
        taken = choose(jnp.broadcast_to(column, (8, piece)) < 0, rim_rows, parts[0])
        factor = taken[species + 1 : species + 2]
        comp_value = comp[:, span]
        mixed[0:species, span] = comp_value - factor * (comp_value - taken[0:species])

    def tests(span):
        levels = jnp.broadcast_to(level[:, span], (8, piece))
        return levels == 2, levels == 0

    def drive(span):
        first, rest = act(left_rate[...], mixed[:, span], *tests(span))
        source[:, span] = jnp.tanh(jnp.concatenate([first, rest], 0))

    def finish(span):
        full, lowest = tests(span)
        first, rest = act(left_implicit[...], source[:, span], full, lowest)
        rest = choose(full, rest, jnp.zeros_like(rest))
        updated = mixed[:, span] + chem_step * jnp.concatenate([first, rest], 0)
        result[:, span] = updated[0:species]

    count = particles // piece
    spans = [slice(k * piece, (k + 1) * piece) for k in range(count)]
    for k in range(count + 2):
        if k < count:
            gather(spans[k])
        if 0 <= k - 1 < count:
            drive(spans[k - 1])
        if 0 <= k - 2:
            finish(spans[k - 2])
            if (k - 1) * piece % group == 0:
                copy((k - 1) * piece // group - 1).start()
        if k == 1:
            for x in range(block_x):
                staged[:, x, :] = table[x + R, 0:species, :]
            send_means = pltpu.make_async_copy(staged, means, done_means)
            send_means.start()
    send_means.wait()
    for k in range(particles // group):
        copy(k).wait()


def per_device(
    counts, composition, particle_mass, particle_cell, particle_level,
    les_mean, mix_rate, rate_matrix, implicit_map,
):
    species, particles = composition.shape
    block_x, block_y = les_mean.shape[1], les_mean.shape[2]
    span_x = block_x + 2 * R
    whole = pl.BlockSpec(memory_space=pltpu.VMEM)
    chunk = 2048
    hbm = pl.BlockSpec(memory_space=pltpu.HBM)
    inputs = composition, particle_mass[None], particle_cell, les_mean, mix_rate
    stay = [pltpu.with_memory_space_constraint(x, pltpu.HBM) for x in inputs]
    dma = pltpu.SemaphoreType.DMA
    tiles = (span_x + 1, ROWS, LANES)
    table, composition, particle_cell = pl.pallas_call(
        functools.partial(sums_kernel, counts, chunk, 512, block_x, block_y),
        out_shape=(
            pltpu.VMEM(tiles, F32),
            pltpu.VMEM(composition.shape, F32),
            pltpu.VMEM(particle_cell.shape, jnp.int32),
        ),
        in_specs=[hbm] * 5,
        out_specs=[whole] * 3,
        scratch_shapes=[
            pltpu.VMEM((1, particles), F32),
            pltpu.VMEM((8, particles), F32),
            pltpu.VMEM(les_mean.shape, F32),
            pltpu.VMEM(mix_rate.shape, F32),
            pltpu.VMEM((2 * block_y, particles), BF),
            pltpu.VMEM((1, particles), F32),
            pltpu.VMEM(((span_x // 2 + 2) * 2 * ROWS, particles), BF),
            pltpu.VMEM(((span_x // 4 + 1) * 2 * ROWS, 2 * block_y), F32),
            pltpu.VMEM((span_x, ROWS, LANES), F32),
            pltpu.VMEM((2, FOLD, LANES), F32),
            pltpu.VMEM((span_x, ROWS, block_y), F32),
            pltpu.VMEM((block_x, ROWS, block_y), F32),
            pltpu.VMEM((2, W, ROWS, LANES), F32),
            pltpu.VMEM((2, 2, FOLD, LANES), F32),
            pltpu.VMEM((2, FOLD, LANES), F32),
            pltpu.VMEM((2, 2, FOLD, LANES), F32),
            dma((particles // chunk,)), dma((4,)), dma((2,)), dma((2,)), dma((8,)), dma((8,)),
        ],
        compiler_params=pltpu.CompilerParams(
            collective_id=0, has_side_effects=True, vmem_limit_bytes=40 << 20
        ),
    )(*stay)
    piece = 512
    group = 2048
    return pl.pallas_call(
        functools.partial(react_kernel, block_x, block_y, piece, group),
        out_shape=(
            jax.ShapeDtypeStruct(composition.shape, F32),
            jax.ShapeDtypeStruct(les_mean.shape, F32),
        ),
        in_specs=[whole] * 6,
        out_specs=[pl.BlockSpec(memory_space=pl.ANY)] * 2,
        scratch_shapes=[
            pltpu.VMEM((span_x // 2 * ROWS, 4 * block_y), BF),
            pltpu.VMEM((ROWS, LANES), BF),
            pltpu.VMEM((ROWS, particles), F32),
            pltpu.VMEM(composition.shape, F32),
            pltpu.VMEM((STACK, ROWS), F32),
            pltpu.VMEM((STACK, ROWS), F32),
            dma((particles // group,)),
            dma(()),
            pltpu.VMEM(les_mean.shape, F32),
            pltpu.VMEM((ROWS, particles), F32),
            pltpu.VMEM((STACK, 3 * ROWS), BF),
            pltpu.VMEM((STACK, 3 * ROWS), BF),
        ],
        compiler_params=pltpu.CompilerParams(vmem_limit_bytes=40 << 20),
    )(composition, particle_cell, particle_level[None], table, rate_matrix, implicit_map)


def solution(mesh):
    placed = (
        P(None, ("gx", "gy")),
        P(("gx", "gy")),
        P(None, ("gx", "gy")),
        P(("gx", "gy")),
        P(None, "gx", "gy"),
        P("gx", "gy"),
        P(),
        P(),
    )
    return jax.shard_map(
        functools.partial(per_device, (mesh.shape["gx"], mesh.shape["gy"])),
        mesh=mesh,
        in_specs=placed,
        out_specs=(P(None, ("gx", "gy")), P(None, "gx", "gy")),
        check_vma=False,
    )
```

```python
import functools

import jax
import jax.numpy as jnp
from jax import lax
from jax.experimental import pallas as pl
from jax.experimental.pallas import tpu as pltpu
from jax.sharding import PartitionSpec as P

NS_LOW = 21
NS_MID = 24
R = 2
W = 2 * R
HALF = 64
ROWS = 56
LANES = 128
STACK = 112
FOLD = 16

prior_weight = 16.0
chem_step = 0.5
BF = jnp.bfloat16
F32 = jnp.float32
MESH = pl.DeviceIdType.MESH


def halves(value):
    high = value.astype(BF)
    return high, (value - high.astype(F32)).astype(BF)


def roll(value, shift):
    return pltpu.roll(value, shift % value.shape[1], 1)


def positions(cell, block_x, block_y):
    local_x = cell[0:1] - (lax.axis_index("gx") * block_x - R)
    local_y = cell[1:2] - (lax.axis_index("gy") * block_y - R)
    low_rim = local_y < W
    on_rim = low_rim | (local_y >= block_y)
    rim = jnp.where(low_rim, local_y, local_y - block_y + (block_x + 2 * R) * W) + local_x * W
    return local_x, on_rim, rim, local_y - R


def one_hot(place, rows):
    sub = lax.broadcasted_iota(jnp.int32, (rows, place.shape[1]), 0)
    same = sub.astype(F32).astype(BF) == jnp.broadcast_to(
        place.astype(F32), (rows, place.shape[1])
    ).astype(BF)
    return jnp.where(same, jnp.ones((), BF), jnp.zeros((), BF))


def prior_of(x, species, les, rate):
    mass = jnp.full((1, LANES), prior_weight, F32)
    fade = 1.0 - jnp.exp(-rate[x : x + 1, :])
    rest = jnp.zeros((ROWS - species - 2, LANES), F32)
    return jnp.concatenate([prior_weight * les[:, x, :], mass, fade, rest], 0)


def sums_kernel(
    counts, chunk, piece, block_x, block_y, comp, mass, cell_in, les_in, rate_in, table, data, cell,
    weight, ending, les, rate, hot, codes, masked, acc, send, edge, prior, plain, from_x, rim_x, from_y, from_xy,
    comp_sem, small_sem, send_main, recv_main, send_rim, recv_rim,
):
    species, particles = comp.shape
    span_x = block_x + 2 * R
    pairs = span_x // 2
    side_size = span_x * W
    folds = LANES // side_size
    tall = 2 * ROWS
    chunks = particles // chunk
    base8 = species // 8 * 8
    early = list(range(0, pairs, 2)) + [pairs]
    late = list(range(1, pairs, 2))
    rows = len(early) * tall
    gx, gy = lax.axis_index("gx"), lax.axis_index("gy")
    has = {
        -1: (gx > 0, gy > 0),
        1: (gx < counts[0] - 1, gy < counts[1] - 1),
        0: (True, True),
    }
    others = [(dx, dy) for dx in (-1, 0, 1) for dy in (-1, 0, 1) if (dx, dy) != (0, 0)]
    lane = lax.broadcasted_iota(jnp.int32, (ROWS, LANES), 1)
    row = lax.broadcasted_iota(jnp.int32, (ROWS, LANES), 0)
    inside = (lane >= R) & (lane < block_y - R)

    def chunk_copy(k):
        span = pl.ds(k * chunk, chunk)
        return pltpu.make_async_copy(
            comp.at[:, span], data.at[:, span], comp_sem.at[k]
        )

    small = [
        pltpu.make_async_copy(cell_in, cell, small_sem.at[0]),
        pltpu.make_async_copy(mass, weight, small_sem.at[1]),
        pltpu.make_async_copy(les_in, les, small_sem.at[2]),
        pltpu.make_async_copy(rate_in, rate, small_sem.at[3]),
    ]
    small[0].start()
    small[1].start()
    for k in range(chunks):
        chunk_copy(k).start()
    small[2].start()
    small[3].start()

    def present(dx, dy):
        return jnp.logical_and(has[dx][0], has[dy][1])

    def landing(dx, dy):
        if dy == 0:
            return rim_x.at[(dx + 1) // 2]
        if dx == 0:
            return from_y.at[(dy + 1) // 2]
        return from_xy.at[(dx + 1) // 2, (dy + 1) // 2]

    def main_copy(dx, phase):
        first = 0 if dx < 0 else block_x
        return pltpu.make_async_remote_copy(
            src_ref=send.at[pl.ds(first + R * phase, R)],
            dst_ref=from_x.at[(1 - dx) // 2, pl.ds(R * phase, R)],
            send_sem=send_main.at[(dx + 1) // 2, phase],
            recv_sem=recv_main.at[(1 - dx) // 2, phase],
            device_id=(gx + dx, gy),
            device_id_type=MESH,
        )

    def rim_copy(k, dx, dy):
        return pltpu.make_async_remote_copy(
            src_ref=edge if dy == 0 else edge.at[(dy + 1) // 2],
            dst_ref=landing(-dx, -dy),
            send_sem=send_rim.at[k],
            recv_sem=recv_rim.at[len(others) - 1 - k],
            device_id=(gx + dx, gy + dy),
            device_id_type=MESH,
        )

    def main_arrival(dx, phase):
        return pltpu.make_async_remote_copy(
            src_ref=send.at[pl.ds(R * phase, R)],
            dst_ref=from_x.at[(dx + 1) // 2, pl.ds(R * phase, R)],
            send_sem=send_main.at[(dx + 1) // 2, phase],
            recv_sem=recv_main.at[(dx + 1) // 2, phase],
            device_id=(gx + dx, gy),
            device_id_type=MESH,
        )

    def rim_arrival(k, dx, dy):
        return pltpu.make_async_remote_copy(
            src_ref=edge if dy == 0 else edge.at[(dy + 1) // 2],
            dst_ref=landing(dx, dy),
            send_sem=send_rim.at[k],
            recv_sem=recv_rim.at[k],
            device_id=(gx + dx, gy + dy),
            device_id_type=MESH,
        )

    barrier = pltpu.get_barrier_semaphore()
    for dx, dy in others:
        @pl.when(present(dx, dy))
        def _():
            pl.semaphore_signal(
                barrier, inc=1, device_id=(gx + dx, gy + dy), device_id_type=MESH
            )
    ending[species - base8 :, :] = jnp.zeros((ROWS - species, particles), F32)
    prior[...] = jnp.zeros_like(prior)
    masked[2 * rows - tall :, :] = jnp.zeros((tall, particles), BF)
    for dx in (-1, 1):
        @pl.when(jnp.logical_not(has[dx][0]))
        def _():
            from_x[(dx + 1) // 2] = jnp.zeros((W, ROWS, LANES), F32)
    for dx, dy in others:
        @pl.when(jnp.logical_not(present(dx, dy)))
        def _():
            landing(dx, dy)[...] = jnp.zeros(landing(dx, dy).shape, F32)

    def total_of(at, cols):
        low, high = slice(at, at + ROWS), slice(at + ROWS, at + tall)
        return acc[low, cols] + acc[high, cols]

    def phase_tiles(phase):
        for u in range(W):
            cols = slice((u % 2) * block_y, (u % 2 + 1) * block_y)
            t = u // 2 * block_x + R * phase + u % 2
            send[t] = total_of(u // 2 * tall, cols) + prior[t]

    def place(at):
        span = slice(at, at + piece)
        local_x, on_rim, rim, inner = positions(cell[:, span], block_x, block_y)
        hot[:, span] = one_hot(
            jnp.where(on_rim, rim, inner + (local_x % 2) * block_y), 2 * block_y
        )
        code = jnp.where(on_rim, pairs, local_x // 2)
        codes[:, span] = code.astype(F32)

    def prepare(at):
        span = slice(at, at + piece)
        mass_here = weight[:, span]
        ending[0 : species - base8, span] = data[base8:, span] * mass_here
        ending[species - base8 : species - base8 + 1, span] = mass_here
        value = jnp.concatenate([data[0:base8, span] * mass_here, ending[:, span]], 0)
        high = value.astype(BF).astype(F32)
        value = jnp.concatenate([high, value - high], 0).astype(BF)
        code = jnp.broadcast_to(codes[:, span], (16, piece)).astype(BF)
        for i, group in enumerate(early + late):
            keep = jnp.where(code == group, jnp.ones((), BF), jnp.zeros((), BF))
            masked[i * tall : (i + 1) * tall, span] = value * jnp.concatenate(
                [keep] * (tall // 16), 0
            )

    def set_prior():
        small[2].wait()
        small[3].wait()
        for x in range(block_x):
            own = prior_of(x, species, les, rate)
            plain[x] = own
            prior[x + R] = jnp.where(inside, own, 0.0)

    small[0].wait()
    for at in range(0, particles, piece):
        place(at)
    small[1].wait()
    for k in range(chunks):
        chunk_copy(k).wait()
        for at in range(k * chunk, (k + 1) * chunk, piece):
            prepare(at)

    set_prior()
    number = (1 + (gx > 0).astype(jnp.int32) + (gx < counts[0] - 1).astype(jnp.int32)) * (
        1 + (gy > 0).astype(jnp.int32) + (gy < counts[1] - 1).astype(jnp.int32)
    ) - 1

    @pl.loop(0, 2)
    def _(phase):
        top = pl.ds(pl.multiple_of(phase * rows, 16), rows)
        acc[...] = lax.dot_general(
            masked[top, :], hot[...], (((1,), (1,)), ((), ())), preferred_element_type=F32
        )
        phase_tiles(phase)

        @pl.when(phase == 0)
        def _():
            pl.semaphore_wait(barrier, number)

        for dx in (-1, 1):
            @pl.when(has[dx][0])
            def _():
                main_copy(dx, phase).start()

        @pl.when(phase == 0)
        def _():
            rim_sum = total_of(pairs // 2 * tall, slice(0, LANES))
            for x in range(block_x):
                t = x + R
                low_at, high_at = t * W + R, side_size + t * W
                low, high = roll(plain[x], low_at), roll(plain[x], high_at + R)
                rim_sum += jnp.where((lane >= low_at) & (lane < low_at + R), low, 0.0)
                rim_sum += jnp.where((lane >= high_at) & (lane < high_at + R), high, 0.0)
            rim_sum = jnp.concatenate([rim_sum, jnp.zeros((folds * FOLD - ROWS, LANES), F32)], 0)
            fold_lane = lax.broadcasted_iota(jnp.int32, (FOLD, LANES), 1)
            for side in range(2):
                packed = jnp.zeros((FOLD, LANES), F32)
                for q in range(folds):
                    moved = roll(rim_sum[q * FOLD : (q + 1) * FOLD], (q - side) * side_size)
                    packed = jnp.where(fold_lane // side_size == q, moved, packed)
                edge[side] = packed
            for k, (dx, dy) in enumerate(others):
                @pl.when(present(dx, dy))
                def _():
                    rim_copy(k, dx, dy).start()

    for k, (dx, dy) in enumerate(others):
        @pl.when(present(dx, dy))
        def _():
            rim_arrival(k, dx, dy).wait_recv()

    def finish(total):
        total_mass = total[species : species + 1, :]
        weight = jnp.where(total_mass > 0.0, total_mass, 1.0)
        weight = jnp.broadcast_to(weight, total.shape)
        return total / jnp.where(row < species, weight, 1.0)

    fold_lane = lax.broadcasted_iota(jnp.int32, (FOLD, LANES), 1)
    place_x = fold_lane % side_size
    sides = []
    for side in range(2):
        total = edge[side]
        for dx, dy in others:
            if dy == 0:
                other = rim_x[(dx + 1) // 2, side]
            elif (dy + 1) // 2 == side:
                other = landing(dx, dy)[...]
            else:
                continue
            if dx < 0:
                other = jnp.where(place_x < 2 * R * W, roll(other, dx * block_x * W), 0.0)
            if dx > 0:
                other = jnp.where(place_x >= block_x * W, roll(other, dx * block_x * W), 0.0)
            total = total + other
        sides.append(total)
    parts = []
    for q in range(folds):
        low, high = roll(sides[0], -q * side_size), roll(sides[1], (1 - q) * side_size)
        parts.append(jnp.where(fold_lane < side_size, low, high))
    total = jnp.where(lane < 2 * side_size, jnp.concatenate(parts, 0)[0:ROWS], 0.0)
    rim_value = finish(total)
    table[span_x] = rim_value

    def close(t):
        side, u = t // W, t % W
        value = finish(send[t] + from_x[side, u])
        if R <= t < R + block_x:
            low_at, high_at = t * W + R, side_size + t * W
            value = jnp.where(lane < R, roll(rim_value, -low_at), value)
            value = jnp.where(
                lane >= block_y - R, roll(rim_value, block_y - R - high_at), value
            )
        table[t] = value

    for phase in range(2):
        for dx in (-1, 1):
            @pl.when(has[dx][0])
            def _():
                main_arrival(dx, phase).wait_recv()

        for side in range(2):
            for u in range(R):
                close(side * block_x + R * phase + u)

    for k, (dx, dy) in enumerate(others):
        @pl.when(present(dx, dy))
        def _():
            rim_copy(k, dx, dy).wait_send()
    for dx in (-1, 1):
        @pl.when(has[dx][0])
        def _():
            for phase in range(2):
                main_copy(dx, phase).wait_send()


def stack_levels(plain, matrices):
    species = matrices.shape[1]
    plain[...] = jnp.zeros_like(plain)
    plain[0:species, 0:species] = matrices[2]
    plain[ROWS : ROWS + NS_MID, 0:NS_MID] = matrices[1, 0:NS_MID, 0:NS_MID]
    base = ROWS + NS_MID
    plain[base : base + NS_LOW, 0:NS_LOW] = matrices[0, 0:NS_LOW, 0:NS_LOW]
    high = plain[...].astype(BF).astype(F32)
    return jnp.concatenate([high, high, plain[...] - high], 1).astype(BF)


def react_kernel(
    block_x, block_y, piece, group, comp, cell, level, table, rate, implicit, out, means,
    left, left_rim, mixed, result, plain_rate, plain_implicit, done, done_means, staged,
    source, left_rate, left_implicit,
):
    species = comp.shape[0]
    particles = comp.shape[1]
    span_x = block_x + 2 * R
    pairs = span_x // 2
    for parity in range(2):
        value = jnp.concatenate([table[2 * g + parity] for g in range(pairs)], 0)
        high, low = halves(value)
        left[:, parity * block_y : (parity + 1) * block_y] = high
        left[:, (2 + parity) * block_y : (3 + parity) * block_y] = low
    value = table[span_x]
    high = value.astype(BF).astype(F32)
    lane = lax.broadcasted_iota(jnp.int32, value.shape, 1)
    low = roll(value - high, HALF)
    left_rim[...] = jnp.where(lane < HALF, high, low).astype(BF)
    mixed[species:, :] = jnp.zeros((ROWS - species, particles), F32)
    left_rate[...] = stack_levels(plain_rate, rate)
    left_implicit[...] = stack_levels(plain_implicit, implicit)

    def choose(test, yes, no):
        shape = (yes.shape[0] // 8, 8, piece)
        return jnp.where(test[None], yes.reshape(shape), no.reshape(shape)).reshape(yes.shape)

    def act(matrix, value, full, lowest):
        high = value.astype(BF).astype(F32)
        right = jnp.concatenate([high, value - high, high], 0).astype(BF)
        got = jnp.dot(matrix, right, preferred_element_type=F32)
        base = ROWS + NS_MID
        first = choose(lowest, got[base : base + NS_MID], got[ROWS:base])
        return choose(full, got[0:NS_MID], first), got[NS_MID:ROWS]

    def copy(k):
        span = pl.ds(k * group, group)
        return pltpu.make_async_copy(result.at[:, span], out.at[:, span], done.at[k])

    def gather(span):
        local_x, on_rim, rim, inner = positions(cell[:, span], block_x, block_y)
        column = jnp.where(on_rim, -1, inner + (local_x % 2) * block_y)
        rim = jnp.where(on_rim, rim, -1)
        hot = one_hot(column, 2 * block_y)
        hot_rim = one_hot(rim, HALF)
        rows = jnp.dot(left[...], jnp.concatenate([hot, hot], 0), preferred_element_type=F32)
        rim_rows = jnp.dot(
            left_rim[...], jnp.concatenate([hot_rim, hot_rim], 0), preferred_element_type=F32
        )
        place = jnp.broadcast_to(local_x // 2, (8, piece))
        parts = [rows[g * ROWS : (g + 1) * ROWS] for g in range(pairs)]
        bit = 1
        while len(parts) > 1:
            test = (place & bit) != 0
            paired = [
                choose(test, parts[i + 1], parts[i]) for i in range(0, len(parts) - 1, 2)
            ]
            parts = paired + parts[2 * len(paired) :]
            bit *= 2
        taken = choose(jnp.broadcast_to(column, (8, piece)) < 0, rim_rows, parts[0])
        factor = taken[species + 1 : species + 2]
        comp_value = comp[:, span]
        mixed[0:species, span] = comp_value - factor * (comp_value - taken[0:species])

    def tests(span):
        levels = jnp.broadcast_to(level[:, span], (8, piece))
        return levels == 2, levels == 0

    def drive(span):
        first, rest = act(left_rate[...], mixed[:, span], *tests(span))
        source[:, span] = jnp.tanh(jnp.concatenate([first, rest], 0))

    def finish(span):
        full, lowest = tests(span)
        first, rest = act(left_implicit[...], source[:, span], full, lowest)
        rest = choose(full, rest, jnp.zeros_like(rest))
        updated = mixed[:, span] + chem_step * jnp.concatenate([first, rest], 0)
        result[:, span] = updated[0:species]

    count = particles // piece
    spans = [slice(k * piece, (k + 1) * piece) for k in range(count)]
    for k in range(count + 2):
        if k < count:
            gather(spans[k])
        if 0 <= k - 1 < count:
            drive(spans[k - 1])
        if 0 <= k - 2:
            finish(spans[k - 2])
            if (k - 1) * piece % group == 0:
                copy((k - 1) * piece // group - 1).start()
        if k == 1:
            for x in range(block_x):
                staged[:, x, :] = table[x + R, 0:species, :]
            send_means = pltpu.make_async_copy(staged, means, done_means)
            send_means.start()
    send_means.wait()
    for k in range(particles // group):
        copy(k).wait()


def per_device(
    counts, composition, particle_mass, particle_cell, particle_level,
    les_mean, mix_rate, rate_matrix, implicit_map,
):
    species, particles = composition.shape
    block_x, block_y = les_mean.shape[1], les_mean.shape[2]
    span_x = block_x + 2 * R
    whole = pl.BlockSpec(memory_space=pltpu.VMEM)
    chunk = 2048
    hbm = pl.BlockSpec(memory_space=pltpu.HBM)
    inputs = composition, particle_mass[None], particle_cell, les_mean, mix_rate
    stay = [pltpu.with_memory_space_constraint(x, pltpu.HBM) for x in inputs]
    dma = pltpu.SemaphoreType.DMA
    tiles = (span_x + 1, ROWS, LANES)
    table, composition, particle_cell = pl.pallas_call(
        functools.partial(sums_kernel, counts, chunk, 512, block_x, block_y),
        out_shape=(
            pltpu.VMEM(tiles, F32),
            pltpu.VMEM(composition.shape, F32),
            pltpu.VMEM(particle_cell.shape, jnp.int32),
        ),
        in_specs=[hbm] * 5,
        out_specs=[whole] * 3,
        scratch_shapes=[
            pltpu.VMEM((1, particles), F32),
            pltpu.VMEM((8, particles), F32),
            pltpu.VMEM(les_mean.shape, F32),
            pltpu.VMEM(mix_rate.shape, F32),
            pltpu.VMEM((2 * block_y, particles), BF),
            pltpu.VMEM((1, particles), F32),
            pltpu.VMEM(((span_x // 2 + 2) * 2 * ROWS, particles), BF),
            pltpu.VMEM(((span_x // 4 + 1) * 2 * ROWS, 2 * block_y), F32),
            pltpu.VMEM((span_x, ROWS, LANES), F32),
            pltpu.VMEM((2, FOLD, LANES), F32),
            pltpu.VMEM((span_x, ROWS, block_y), F32),
            pltpu.VMEM((block_x, ROWS, block_y), F32),
            pltpu.VMEM((2, W, ROWS, LANES), F32),
            pltpu.VMEM((2, 2, FOLD, LANES), F32),
            pltpu.VMEM((2, FOLD, LANES), F32),
            pltpu.VMEM((2, 2, FOLD, LANES), F32),
            dma((particles // chunk,)), dma((4,)), dma((2, 2)), dma((2, 2)), dma((8,)), dma((8,)),
        ],
        compiler_params=pltpu.CompilerParams(
            collective_id=0, has_side_effects=True, vmem_limit_bytes=40 << 20
        ),
    )(*stay)
    piece = 512
    group = 2048
    return pl.pallas_call(
        functools.partial(react_kernel, block_x, block_y, piece, group),
        out_shape=(
            jax.ShapeDtypeStruct(composition.shape, F32),
            jax.ShapeDtypeStruct(les_mean.shape, F32),
        ),
        in_specs=[whole] * 6,
        out_specs=[pl.BlockSpec(memory_space=pl.ANY)] * 2,
        scratch_shapes=[
            pltpu.VMEM((span_x // 2 * ROWS, 4 * block_y), BF),
            pltpu.VMEM((ROWS, LANES), BF),
            pltpu.VMEM((ROWS, particles), F32),
            pltpu.VMEM(composition.shape, F32),
            pltpu.VMEM((STACK, ROWS), F32),
            pltpu.VMEM((STACK, ROWS), F32),
            dma((particles // group,)),
            dma(()),
            pltpu.VMEM(les_mean.shape, F32),
            pltpu.VMEM((ROWS, particles), F32),
            pltpu.VMEM((STACK, 3 * ROWS), BF),
            pltpu.VMEM((STACK, 3 * ROWS), BF),
        ],
        compiler_params=pltpu.CompilerParams(vmem_limit_bytes=40 << 20),
    )(composition, particle_cell, particle_level[None], table, rate_matrix, implicit_map)


def solution(mesh):
    placed = (
        P(None, ("gx", "gy")),
        P(("gx", "gy")),
        P(None, ("gx", "gy")),
        P(("gx", "gy")),
        P(None, "gx", "gy"),
        P("gx", "gy"),
        P(),
        P(),
    )
    return jax.shard_map(
        functools.partial(per_device, (mesh.shape["gx"], mesh.shape["gy"])),
        mesh=mesh,
        in_specs=placed,
        out_specs=(P(None, ("gx", "gy")), P(None, "gx", "gy")),
        check_vma=False,
    )
```
